256 devices in a mesh: grp: 16 (over z, core), pool: 16 (over y, x).
Axes of the slice: x: 4, y: 4, z: 8, core: 2. Of those that a mesh axis runs over, the one named last changes fastest.
Arguments:
- tokens: bfloat16 [16, 2048, 2048], P('grp', 'pool'), may hold values from -6 to 6
- ln_gain: bfloat16 [2048], replicated, may hold values from 0.099609375 to 1.8984375
- w_qkv: bfloat16 [2048, 16, 192], P('grp', 'pool'), may hold values from -0.25 to 0.25
- w_out: bfloat16 [16, 64, 2048], P('pool', None, 'grp'), may hold values from -0.1875 to 0.1875
- w_fc: bfloat16 [2048, 8192], P(None, 'pool'), may hold values from -0.125 to 0.125
- w_proj: bfloat16 [8192, 2048], P('pool'), may hold values from -0.0625 to 0.0625
- pool_kv: bfloat16 [16, 256, 16, 16, 128], P('grp', 'pool'), may hold values from -160 to 160, as said below
- block_table: int32 [16, 8, 128], P('grp'), may hold values from 0 to 255, as said below
- block_count: int32 [16, 8], P('grp'), may hold values from 1 to 128, as said below
- lengths: int32 [16, 8], P('grp'), may hold values from 1 to 512, 2048 in all within a row
Outputs:
- layer_out: bfloat16 [16, 2048, 2048], P('grp', 'pool')
The draws below stay inside these ranges and needn't reach their ends.
Inputs may be any that keep to these rules, and one draw needn't show every extreme that they name: `block_table`: the first block_count entries of a request's row are distinct; later entries are valid block numbers and are not used. `block_count`: in every group some request uses 128 blocks. `pool_kv`: in the last dimension the first 64 entries are a head's key, already rotated, and the last 64 its value.
All inputs are finite; a program needn't handle non-finite values.
Results may differ from the reference program's by a relative error of at most 0.017.
Values may be sent and summed in bfloat16 or wider, within the bound.
No kernel may reach another device: no remote copies, remote signals or barrier semaphores. Data moves between devices by JAX's collectives and lax.ppermute only.
A program may use at most 128 MiB of HBM per device.

```python
import math
import jax
import jax.numpy as jnp
import numpy as np
from jax import lax

D = 2048
HD = 64
FF = 8192
ROT = 32
H = 16
BS = 16
REQ = 8
GROUP_TOK = 2048
POOL_BLOCKS = 256
MAXB = 128
N_GRP = 16
N_POOL = 16


def draw_pool_kv(key, part):
    shape = (N_GRP, POOL_BLOCKS, BS, H, 2 * HD)
    return (2.0 * jax.random.truncated_normal(jax.random.fold_in(key, 1), -6.0, 6.0, shape, jnp.float32)).astype(jnp.bfloat16)


def draw_block_table(key, part):
    scores = jax.random.randint(jax.random.fold_in(key, 11), (N_GRP, REQ, POOL_BLOCKS), 0, 2 ** 18)
    distinct = scores * POOL_BLOCKS + jnp.arange(POOL_BLOCKS, dtype=jnp.int32)[None, None, :]
    order = jnp.argsort(distinct, axis=-1)
    return order[..., :MAXB].astype(jnp.int32)


def draw_block_count(key, part):
    counts = jax.random.randint(jax.random.fold_in(key, 12), (N_GRP, REQ), 1, MAXB + 1)
    chosen = jax.random.randint(jax.random.fold_in(key, 13), (N_GRP, 1), 0, REQ)
    return jnp.where(jnp.arange(REQ, dtype=jnp.int32)[None, :] == chosen, MAXB, counts).astype(jnp.int32)


def block_scale(rng, shape, shards, smallest, largest):
    def one(dim, blocks):
        heights = jax.random.uniform(jax.random.fold_in(jax.random.fold_in(rng, 6), dim), (blocks,), jnp.float32, smallest / len(shards), largest / len(shards))
        return jnp.repeat(jnp.exp(heights), shape[dim] // blocks).reshape((-1,) + (1,) * (len(shape) - dim - 1))

    level = one(*shards[0])
    for cut in shards[1:]:
        level = level * one(*cut)
    return level


def split_up(amount, total, reach, lean):
    weights = [(1 << 20) // math.isqrt(standing ** lean) + 1 for standing in range(2, amount + 1)]
    surplus, holding = total - reach - (amount - 1), [1] * (amount - 1)
    while surplus > 0:
        free = [i for i in range(amount - 1) if holding[i] < reach]
        whole, budget = sum([weights[i] for i in free]), surplus
        for i in free:
            more = min(reach - holding[i], max(1, budget * weights[i] // whole), surplus)
            holding[i] = holding[i] + more
            surplus = surplus - more
    return np.array([reach] + holding)


def ragged_sizes(stream_key, count, total, most, slope):
    if count == 2:
        one = jax.random.randint(stream_key, (), max(1, total - most), min(most, total - 1) + 1)
        return jnp.stack([one, total - one])
    tallies = jnp.asarray(split_up(count, total, most, slope), jnp.int32)
    pairs = (count - 1) // 2
    giver, receiver = tallies[1:1 + 2 * pairs:2], tallies[2:2 + 2 * pairs:2]
    margin = jnp.minimum(giver - 1, most - receiver)
    moved = jax.random.randint(jax.random.fold_in(stream_key, 1), (pairs,), 0, 1 << 20) % (margin + 1)
    tallies = tallies.at[1:1 + 2 * pairs:2].set(giver - moved).at[2:2 + 2 * pairs:2].set(receiver + moved)
    return tallies[jax.random.permutation(jax.random.fold_in(stream_key, 2), count)]


def gaussian(stream_key, extent, deviation, most, split=(), kind=jnp.bfloat16):
    drawn = jax.random.normal(stream_key, extent, jnp.float32) * deviation
    if len(split) > 0:
        drawn = block_scale(stream_key, extent, split, -0.22, 0.18) * drawn
    return jnp.clip(drawn, min=-most, max=most).astype(kind)


def setup_inputs(seed: int = 0) -> dict:
    seeds = jax.random.split(jax.random.key(seed), 11)
    tokens = gaussian(seeds[0], (N_GRP, GROUP_TOK, D), 1.0, 6.0, ((0, 16), (1, 16)))
    ln_gain = jnp.clip(1.0 + 0.18 * jax.random.normal(seeds[1], (D,), jnp.float32), 0.099609375, 1.8984375).astype(jnp.bfloat16)
    w_qkv = gaussian(seeds[2], (D, H, 3 * HD), (D // 4) ** -0.5, 0.25, ((0, 16), (1, 16)))
    w_out = gaussian(seeds[3], (H, HD, D), (H * HD) ** -0.5, 0.1875, ((0, 16), (2, 16)))
    w_fc = gaussian(seeds[4], (D, FF), D ** -0.5, 0.125, ((1, 16),))
    w_proj = gaussian(seeds[5], (FF, D), FF ** -0.5, 0.0625, ((0, 16),))
    pool_kv = draw_pool_kv(jax.random.fold_in(seeds[10], 71), 0)
    block_table = draw_block_table(jax.random.fold_in(seeds[10], 71), 0)
    block_count = draw_block_count(jax.random.fold_in(seeds[10], 71), 0)
    lengths = jax.vmap(lambda own: ragged_sizes(own, REQ, GROUP_TOK, GROUP_TOK // 4, 2))(jax.random.split(seeds[9], N_GRP)).reshape((N_GRP, REQ)).astype(jnp.int32)
    return dict(tokens=tokens, ln_gain=ln_gain, w_qkv=w_qkv, w_out=w_out, w_fc=w_fc, w_proj=w_proj, pool_kv=pool_kv, block_table=block_table, block_count=block_count, lengths=lengths)


epsilon = 1e-05

def layer_norm(rows, gain):
    values = rows.astype(jnp.float32)
    centred = values - lax.optimization_barrier(jnp.mean(values, axis=-1, keepdims=True))
    variance = lax.optimization_barrier(jnp.mean(centred * centred, axis=-1, keepdims=True))
    return (centred * lax.rsqrt(variance + epsilon) * gain.astype(jnp.float32)).astype(jnp.bfloat16)

def rotate(field, where):
    half = ROT // 2
    frequency = 10000.0 ** (-2.0 * jnp.arange(half, dtype=jnp.float32) / ROT)
    angle = where.astype(jnp.float32)[:, None] * frequency[None, :]
    cosine = jnp.cos(angle)[:, None, :]
    sine = jnp.sin(angle)[:, None, :]
    first = field[..., :half]
    second = field[..., half:ROT]
    return jnp.concatenate([first * cosine - second * sine, second * cosine + first * sine, field[..., ROT:]], axis=-1)

def request_info(request_lengths, counts, table, group_tok, pool_blocks, block_len):
    ends = jnp.cumsum(request_lengths).astype(jnp.int32)
    starts = ends - request_lengths
    token_index = jnp.arange(group_tok, dtype=jnp.int32)
    inside = (token_index[:, None] >= starts[None, :]) & (token_index[:, None] < ends[None, :])
    numbers = jnp.arange(request_lengths.shape[0], dtype=jnp.int32)
    request_of = lax.optimization_barrier(jnp.sum(jnp.where(inside, numbers[None, :], 0), axis=-1)).astype(jnp.int32)
    position = lax.optimization_barrier(jnp.sum(jnp.where(inside, (counts * block_len - starts)[None, :], 0), axis=-1)).astype(jnp.int32) + token_index
    listed = jnp.arange(table.shape[1], dtype=jnp.int32)[None, :] < counts[:, None]
    member = jnp.any((table[:, :, None] == jnp.arange(pool_blocks, dtype=jnp.int32)[None, None, :]) & listed[:, :, None], axis=1)
    allowed = jnp.dot(inside.astype(jnp.float32), member.astype(jnp.float32), preferred_element_type=jnp.float32) > 0.5
    return (request_of, position, allowed)

def partial_attention(queries, keys, values, visible):
    scale = queries.shape[-1] ** (-0.5)
    scores = jnp.einsum('rhe,khe->rhk', queries.astype(jnp.float32), keys.astype(jnp.float32)) * scale
    scores = jnp.where(visible[:, None, :], scores, -1e+30)
    highest = lax.optimization_barrier(jnp.max(scores, axis=-1))
    weights = jnp.where(visible[:, None, :], jnp.exp(scores - highest[..., None]), 0.0).astype(jnp.bfloat16)
    total = lax.optimization_barrier(jnp.sum(weights.astype(jnp.float32), axis=-1))
    summed = jnp.einsum('rhk,khe->rhe', weights.astype(jnp.float32), values.astype(jnp.float32))
    return (highest, total, summed)

def reference(tokens, ln_gain, w_qkv, w_out, w_fc, w_proj, pool_kv, block_table, block_count, lengths):
    heads_dev = H // N_POOL
    units_dev = FF // N_POOL
    out_flat = w_out.reshape(H * HD, D)

    def one_group(group):
        rows, pool, table, counts, request_lengths = group
        group_tok = rows.shape[0]
        pool_blocks = pool.shape[0]
        request_of, position, allowed = request_info(request_lengths, counts, table, group_tok, pool_blocks, BS)
        normed = layer_norm(rows, ln_gain)
        projected = jnp.einsum('td,dhe->the', normed.astype(jnp.float32), w_qkv.astype(jnp.float32))
        query = rotate(projected[..., :HD], position).astype(jnp.bfloat16)
        key_new = rotate(projected[..., HD:2 * HD], position).astype(jnp.bfloat16)
        value_new = projected[..., 2 * HD:].astype(jnp.bfloat16)
        hidden = jax.nn.gelu(jnp.dot(normed, w_fc, preferred_element_type=jnp.float32), approximate=True).astype(jnp.bfloat16)
        keys_all = jnp.concatenate([pool[..., :HD].reshape(pool_blocks * BS, H, HD), key_new], axis=0)
        values_all = jnp.concatenate([pool[..., HD:].reshape(pool_blocks * BS, H, HD), value_new], axis=0)
        token_index = jnp.arange(group_tok, dtype=jnp.int32)
        same = (request_of[:, None] == request_of[None, :]) & (token_index[None, :] <= token_index[:, None])
        visible = jnp.concatenate([jnp.repeat(allowed, BS, axis=1), same], axis=1)
        block_rows = min(512, group_tok)

        def attend(block_index):
            begin = block_index * block_rows
            query_rows = lax.dynamic_slice_in_dim(query, begin, block_rows)
            seen = lax.dynamic_slice_in_dim(visible, begin, block_rows)
            highest, total, summed = partial_attention(query_rows, keys_all, values_all, seen)
            return summed / total[..., None]
        attention = lax.map(attend, jnp.arange(group_tok // block_rows, dtype=jnp.int32))
        attention = attention.reshape(group_tok, H * HD).astype(jnp.bfloat16)

        def add_group(carry, holder):
            width = heads_dev * HD
            attn_part = lax.dynamic_slice_in_dim(attention, holder * width, width, 1)
            out_part = lax.dynamic_slice_in_dim(out_flat, holder * width, width, 0)
            hidden_part = lax.dynamic_slice_in_dim(hidden, holder * units_dev, units_dev, 1)
            proj_part = lax.dynamic_slice_in_dim(w_proj, holder * units_dev, units_dev, 0)
            term = jnp.dot(attn_part, out_part, preferred_element_type=jnp.float32) + jnp.dot(hidden_part, proj_part, preferred_element_type=jnp.float32)
            rounded = lax.optimization_barrier(term.astype(jnp.bfloat16))
            return (carry + rounded.astype(jnp.float32), None)
        summed, unused = lax.scan(add_group, jnp.zeros((group_tok, D), jnp.float32), jnp.arange(N_POOL, dtype=jnp.int32))
        return (rows.astype(jnp.float32) + summed).astype(jnp.bfloat16)
    return lax.map(one_group, (tokens, pool_kv, block_table, block_count, lengths))
```

```python
import functools

import jax
import jax.numpy as jnp
from jax import lax
from jax.experimental import pallas as pl
from jax.experimental.pallas import tpu as pltpu
from jax.sharding import PartitionSpec as P

ROT = 32


epsilon = 1e-05


def layer_norm(rows, gain):
    values = rows.astype(jnp.float32)
    centred = values - jnp.mean(values, axis=-1, keepdims=True)
    variance = jnp.mean(centred * centred, axis=-1, keepdims=True)
    return (centred * lax.rsqrt(variance + epsilon) * gain.astype(jnp.float32)).astype(jnp.bfloat16)


def rotate(field, where):
    half = ROT // 2
    frequency = 10000.0 ** (-2.0 * jnp.arange(half, dtype=jnp.float32) / ROT)
    angle = where.astype(jnp.float32)[:, None] * frequency[None, :]
    cosine = jnp.cos(angle)[:, None, :]
    sine = jnp.sin(angle)[:, None, :]
    first = field[..., :half]
    second = field[..., half:ROT]
    return jnp.concatenate(
        [first * cosine - second * sine, second * cosine + first * sine, field[..., ROT:]], axis=-1
    )


def positions(request_lengths, counts, group_tok, block_len):
    ends = jnp.cumsum(request_lengths)
    starts = ends - request_lengths
    token_index = jnp.arange(group_tok, dtype=jnp.int32)
    inside = (token_index[:, None] >= starts[None, :]) & (token_index[:, None] < ends[None, :])
    position = (
        jnp.sum(jnp.where(inside, (counts * block_len - starts)[None, :], 0), axis=-1) + token_index
    )
    return position


LOG2E = 1.4426950408889634


def attention_kernel(
    chunk, span, scale, table_ref, count_ref, length_ref, query_ref, fresh_ref, pool_ref,
    out_ref, key_ref, value_ref
):
    tokens, lanes = query_ref.shape
    head_dim = lanes // 2
    block_len = pool_ref.shape[1]
    requests = table_ref.shape[0]
    per_chunk = chunk // block_len
    factor = scale * LOG2E
    tile = span
    unroll = 8
    block_lane = lax.broadcasted_iota(jnp.int32, (block_len, lanes), 1)
    one = jnp.ones((), jnp.bfloat16)
    nil = jnp.zeros((), jnp.bfloat16)

    def step(carry, query, keys, values, visible):
        highest, acc = carry
        scores = factor * lax.dot_general(
            query, keys, (((1,), (1,)), ((), ())), preferred_element_type=jnp.float32
        )
        if visible is not None:
            scores = jnp.where(visible, scores, -1e30)
        top = jnp.maximum(highest, jnp.max(scores, axis=-1, keepdims=True))
        weights = jnp.exp2(scores - top).astype(jnp.bfloat16)
        acc = acc * jnp.exp2(highest - top) + jnp.dot(
            weights, values, preferred_element_type=jnp.float32
        )
        return top, acc

    def request(r, start):
        length = length_ref[r]
        count = count_ref[r]
        chunks = (count + per_chunk - 1) // per_chunk

        def gather(i, _):
            for u in range(unroll):
                b = i * unroll + u
                block = pool_ref[table_ref[r, jnp.minimum(b, count - 1)]]
                where = pl.ds(pl.multiple_of(b * block_len, block_len), block_len)
                key_ref[where, :] = block
                paired = jnp.where(block_lane < head_dim, one, block)
                value_ref[where, :] = jnp.where(b < count, paired, nil)
            return 0

        lax.fori_loop(0, chunks * (per_chunk // unroll), gather, 0)
        first = start // 16 * 16
        tiles = (start + length - first + tile - 1) // tile

        def one_tile(i, _):
            row = pl.multiple_of(jnp.minimum(first + i * tile, tokens - tile), 16)
            rows = pl.ds(row, tile)
            query = query_ref[rows, :]

            def pooled(j, carry):
                where = pl.ds(pl.multiple_of(j * chunk, chunk), chunk)
                return step(carry, query, key_ref[where, :], value_ref[where, :], None)

            carry = (
                jnp.full((tile, 1), -1e30, jnp.float32),
                jnp.zeros((tile, lanes), jnp.float32),
            )
            carry = lax.fori_loop(0, chunks, pooled, carry)
            own = row + lax.broadcasted_iota(jnp.int32, (tile, span), 0)

            def new(j, carry):
                begin = pl.multiple_of(j * span, span)
                both = fresh_ref[pl.ds(begin, span), :]
                lane = lax.broadcasted_iota(jnp.int32, (span, lanes), 1)
                values = jnp.where(lane < head_dim, one, both)
                other = begin + lax.broadcasted_iota(jnp.int32, (tile, span), 1)
                visible = (other >= start) & (other <= own)
                return step(carry, query, both, values, visible)

            highest, acc = lax.fori_loop(
                start // span, (row + tile + span - 1) // span, new, carry
            )
            result = (acc[:, head_dim:] / acc[:, :head_dim]).astype(jnp.bfloat16)
            place = row + lax.broadcasted_iota(jnp.int32, (tile, head_dim), 0)
            inside = (place >= start) & (place < start + length)
            out_ref[rows, :] = jnp.where(inside, result, out_ref[rows, :])
            return 0

        lax.fori_loop(0, tiles, one_tile, 0)
        return start + length

    lax.fori_loop(0, requests, request, 0)


def attend(query, fresh, pool, table, counts, lengths, chunk=512, span=256):
    tokens, lanes = query.shape
    block_len = pool.shape[1]
    keys = table.shape[1] * block_len
    keys = -(-keys // chunk) * chunk
    head_dim = lanes // 2
    smem = pl.BlockSpec(memory_space=pltpu.SMEM)
    vmem = pl.BlockSpec(memory_space=pltpu.VMEM)
    return pl.pallas_call(
        functools.partial(attention_kernel, chunk, span, head_dim**-0.5),
        out_shape=jax.ShapeDtypeStruct((tokens, head_dim), jnp.bfloat16),
        in_specs=[smem, smem, smem, vmem, vmem, vmem],
        out_specs=vmem,
        scratch_shapes=[
            pltpu.VMEM((keys, lanes), jnp.bfloat16),
            pltpu.VMEM((keys, lanes), jnp.bfloat16),
        ],
        compiler_params=pltpu.CompilerParams(vmem_limit_bytes=24 * 1024 * 1024),
        cost_estimate=pl.CostEstimate(
            flops=2 * tokens * keys * lanes * 2, bytes_accessed=3 * 1024 * 1024,
            transcendentals=tokens * keys,
        ),
        name="attend",
    )(table, counts, lengths, query, fresh, pool)


def per_device(
    tokens, ln_gain, w_qkv, w_out, w_fc, w_proj, pool_kv, block_table, block_count, lengths
):
    holders = lax.axis_size("pool")
    rows_dev = tokens.shape[1]
    group_tok = rows_dev * holders
    local_pool = pool_kv[0]
    blk_dev, block_len, heads_all, paired = local_pool.shape
    head_dim = paired // 2
    pool_blocks = blk_dev * holders
    qkv_weight, out_weight = (
        lax.all_gather(w_qkv, "grp", axis=0, tiled=True),
        lax.all_gather(w_out, "grp", axis=2, tiled=True),
    )
    heads_dev = qkv_weight.shape[1]
    position = positions(lengths[0], block_count[0], group_tok, block_len)
    normed = layer_norm(tokens[0], ln_gain)
    units = w_fc.shape[1]
    piece = lax.all_gather(normed, "pool", axis=0, tiled=True)
    count = piece.shape[0]
    hidden_rows = jax.nn.gelu(
        jnp.dot(piece, w_fc, preferred_element_type=jnp.float32), approximate=True
    ).astype(jnp.bfloat16)
    projected = jnp.einsum("td,dhe->the", piece, qkv_weight, preferred_element_type=jnp.float32)
    query_rows = rotate(projected[..., :head_dim], position)
    key_rows = rotate(projected[..., head_dim : 2 * head_dim], position)
    joined = jnp.concatenate(
        [query_rows, key_rows, projected[..., 2 * head_dim :]], axis=-1
    ).astype(jnp.bfloat16)
    results = jnp.concatenate(
        [hidden_rows, joined.reshape(count, heads_dev * 3 * head_dim)], axis=1
    )
    hidden = results[:, :units]
    joined = results[:, units:].reshape(group_tok, heads_dev, 3 * head_dim)
    query = joined[:, 0, :head_dim]
    query = jnp.concatenate([query, jnp.zeros_like(query)], axis=1)
    fresh = joined[:, 0, head_dim:]
    pooled = lax.all_to_all(local_pool, "pool", split_axis=2, concat_axis=0, tiled=True)
    pooled = pooled.reshape(pool_blocks, block_len, paired)
    attention = attend(query, fresh, pooled, block_table[0], block_count[0], lengths[0])
    attention = attention.reshape(group_tok, heads_dev * head_dim)
    out_rows = out_weight.reshape(heads_dev * head_dim, out_weight.shape[2])
    summed = lax.psum_scatter(
        (
            jnp.dot(attention, out_rows, preferred_element_type=jnp.float32)
            + jnp.dot(hidden, w_proj, preferred_element_type=jnp.float32)
        ).astype(jnp.bfloat16),
        "pool",
        scatter_dimension=0,
        tiled=True,
    ).astype(jnp.float32)
    return (tokens[0].astype(jnp.float32) + summed).astype(jnp.bfloat16)[None]


def solution(mesh):
    in_specs = (
        P("grp", "pool", None),
        P(),
        P("grp", "pool", None),
        P("pool", None, "grp"),
        P(None, "pool"),
        P("pool", None),
        P("grp", "pool", None, None, None),
        P("grp", None, None),
        P("grp", None),
        P("grp", None),
    )
    out_specs = P("grp", "pool", None)
    return jax.shard_map(
        per_device, mesh=mesh, in_specs=in_specs, out_specs=out_specs, check_vma=False
    )
```

```python
import functools

import jax
import jax.numpy as jnp
from jax import lax
from jax.experimental import pallas as pl
from jax.experimental.pallas import tpu as pltpu
from jax.sharding import Mesh
from jax.sharding import PartitionSpec as P

ROT = 32
LOG2E = 1.4426950408889634
MIB = 1024 * 1024
epsilon = 1e-05


def layer_norm(rows, gain):
    values = rows.astype(jnp.float32)
    centred = values - jnp.mean(values, axis=-1, keepdims=True)
    variance = jnp.mean(centred * centred, axis=-1, keepdims=True)
    return (centred * lax.rsqrt(variance + epsilon) * gain.astype(jnp.float32)).astype(jnp.bfloat16)


def rotation_tables(request_lengths, counts, first_token, tokens, block_len, lanes):
    half = ROT // 2
    ends = jnp.cumsum(request_lengths)
    starts = ends - request_lengths
    index = first_token + jnp.arange(tokens, dtype=jnp.int32)
    inside = (index[:, None] >= starts[None, :]) & (index[:, None] < ends[None, :])
    position = (
        jnp.sum(jnp.where(inside, (counts * block_len - starts)[None, :], 0), axis=-1) + index
    )
    frequency = 10000.0 ** (-2.0 * jnp.arange(half, dtype=jnp.float32) / ROT)
    lane = jnp.arange(lanes, dtype=jnp.int32)
    spread = jnp.where(lane < ROT, jnp.tile(frequency, lanes // half), 0.0)
    angle = position.astype(jnp.float32)[:, None] * spread[None, :]
    sine = jnp.sin(angle)
    return jnp.cos(angle), jnp.where(lane[None, :] < half, -sine, sine)


def qkv_kernel(
    place_ref, own_ref, right_ref, low_ref, high_ref, left_ref, weight_ref, cos_ref, sin_ref,
    rows_ref, sent_ref
):
    x, y = place_ref[0], place_ref[1]
    ring = sent_ref.shape[0]
    part = own_ref.shape[0]
    tokens, lanes = cos_ref.shape
    head = lanes // 2

    def put(piece, step, offset):
        begin = pl.multiple_of(lax.rem(x + step, ring) * part + offset, 16)
        rows_ref[pl.ds(begin, piece.shape[0]), :] = piece[...]

    put(own_ref, 0, 0)
    put(right_ref, 1, 0)
    put(low_ref, 2, 0)
    put(high_ref, 2, part // 2)
    put(left_ref, 3, 0)
    lane = lax.broadcasted_iota(jnp.int32, (tokens, lanes), 1)

    def rotated(field):
        other = jnp.where(
            lane < ROT // 2, pltpu.roll(field, lanes - ROT // 2, 1), pltpu.roll(field, ROT // 2, 1)
        )
        return field * cos_ref[...] + other * sin_ref[...]

    def product(begin, size):
        weight = jnp.concatenate(
            [weight_ref[g, begin : begin + size, :] for g in range(weight_ref.shape[0])], axis=1
        )
        return lax.dot_general(
            rows_ref[...], weight, (((1,), (1,)), ((), ())), preferred_element_type=jnp.float32
        )

    for pair in range(ring // 2):
        both = product(pair * 2 * lanes, 2 * lanes)
        for k in range(2):
            target = lax.rem(y + 2 * pair + k, ring)
            field = rotated(both[:, k * lanes : (k + 1) * lanes])
            sent_ref[target, :tokens, :] = field.astype(jnp.bfloat16)
    queries = product(ring * lanes, ring * head)
    for d in range(ring):
        field = queries[:, d // 2 * lanes : (d // 2 + 1) * lanes]
        if d % 2:
            field = pltpu.roll(field, head, 1)
        field = rotated(field)
        top, bottom = field[: tokens // 2], pltpu.roll(field[tokens // 2 :], head, 1)
        folded = jnp.where(lane[: tokens // 2] < head, top, bottom)
        sent_ref[lax.rem(y + d, ring), tokens:, :] = folded.astype(jnp.bfloat16)


def attention_kernel(
    chunk, span, scale, table_ref, count_ref, length_ref, sent_ref, pool_ref, out_ref,
    query_ref, fresh_ref, result_ref, key_ref, value_ref
):
    tokens, lanes = query_ref.shape
    head = lanes // 2
    ring = sent_ref.shape[0]
    part = tokens // ring
    block_len = pool_ref.shape[1]
    requests = table_ref.shape[0]
    per_chunk = chunk // block_len
    factor = scale * LOG2E
    tile = span
    unroll = 8
    block_lane = lax.broadcasted_iota(jnp.int32, (block_len, lanes), 1)
    fold_lane = lax.broadcasted_iota(jnp.int32, (part // 2, lanes), 1)
    one = jnp.ones((), jnp.bfloat16)
    nil = jnp.zeros((), jnp.bfloat16)

    for i in range(ring):
        fresh_ref[i * part : (i + 1) * part, :] = sent_ref[i, :part, :]
        folded = sent_ref[i, part:, :].astype(jnp.float32)
        for k in range(2):
            unfolded = folded if k == 0 else pltpu.roll(folded, head, 1)
            begin = i * part + k * (part // 2)
            query_ref[begin : begin + part // 2, :] = jnp.where(
                fold_lane < head, unfolded, 0.0
            ).astype(jnp.bfloat16)

    def step(carry, query, keys, values, visible):
        highest, acc = carry
        scores = factor * lax.dot_general(
            query, keys, (((1,), (1,)), ((), ())), preferred_element_type=jnp.float32
        )
        if visible is not None:
            scores = jnp.where(visible, scores, -1e30)
        top = jnp.maximum(highest, jnp.max(scores, axis=-1, keepdims=True))
        weights = jnp.exp2(scores - top).astype(jnp.bfloat16)
        acc = acc * jnp.exp2(highest - top) + jnp.dot(
            weights, values, preferred_element_type=jnp.float32
        )
        return top, acc

    def request(r, start):
        length = length_ref[r]
        count = count_ref[r]
        chunks = (count + per_chunk - 1) // per_chunk

        def gather(i, _):
            for u in range(unroll):
                b = i * unroll + u
                block = pool_ref[table_ref[r, jnp.minimum(b, count - 1)]]
                where = pl.ds(pl.multiple_of(b * block_len, block_len), block_len)
                key_ref[where, :] = block
                paired = jnp.where(block_lane < head, one, block)
                value_ref[where, :] = jnp.where(b < count, paired, nil)
            return 0

        lax.fori_loop(0, chunks * (per_chunk // unroll), gather, 0)
        first = start // 16 * 16
        tiles = (start + length - first + tile - 1) // tile

        def one_tile(i, _):
            row = pl.multiple_of(jnp.minimum(first + i * tile, tokens - tile), 16)
            rows = pl.ds(row, tile)
            query = query_ref[rows, :]

            def pooled(j, carry):
                where = pl.ds(pl.multiple_of(j * chunk, chunk), chunk)
                return step(carry, query, key_ref[where, :], value_ref[where, :], None)

            carry = (
                jnp.full((tile, 1), -1e30, jnp.float32),
                jnp.zeros((tile, lanes), jnp.float32),
            )
            carry = lax.fori_loop(0, chunks, pooled, carry)
            own = row + lax.broadcasted_iota(jnp.int32, (tile, span), 0)

            def new(j, carry):
                begin = pl.multiple_of(j * span, span)
                both = fresh_ref[pl.ds(begin, span), :]
                lane = lax.broadcasted_iota(jnp.int32, (span, lanes), 1)
                values = jnp.where(lane < head, one, both)
                other = begin + lax.broadcasted_iota(jnp.int32, (tile, span), 1)
                visible = (other >= start) & (other <= own)
                return step(carry, query, both, values, visible)

            highest, acc = lax.fori_loop(
                start // span, (row + tile + span - 1) // span, new, carry
            )
            result = (acc / pltpu.roll(acc, head, 1)).astype(jnp.bfloat16)
            place = row + lax.broadcasted_iota(jnp.int32, (tile, lanes), 0)
            inside = (place >= start) & (place < start + length)
            result_ref[rows, :] = jnp.where(inside, result, result_ref[rows, :])
            return 0

        lax.fori_loop(0, tiles, one_tile, 0)
        return start + length

    lax.fori_loop(0, requests, request, 0)
    for i in range(ring):
        top = result_ref[i * part : i * part + part // 2, :].astype(jnp.float32)
        bottom = result_ref[i * part + part // 2 : (i + 1) * part, :].astype(jnp.float32)
        out_ref[i] = jnp.where(fold_lane < head, pltpu.roll(top, head, 1), bottom).astype(
            jnp.bfloat16
        )


def gelu(value):
    return jax.nn.gelu(value, approximate=True).astype(jnp.bfloat16)


def mix_kernel(
    place_ref, rows_ref, fc_ref, proj_ref,
    fc_up_ref, fc_up2_ref, proj_up_ref, proj_up2_ref,
    fc_down_ref, fc_down2_ref, proj_down_ref, proj_down2_ref,
    gathered_ref, heads_ref, out_ref, total_ref, hidden_ref
):
    x, core = place_ref[0], place_ref[2]
    tokens, width = rows_ref.shape
    units = fc_ref.shape[1]
    ring, part, _ = out_ref.shape
    groups, _, lanes = gathered_ref.shape
    head = lanes // 2
    stripe = 512

    def dot(a, b):
        return jnp.dot(a, b, preferred_element_type=jnp.float32)

    def add(columns, value, first=False):
        total_ref[:, columns] = value if first else total_ref[:, columns] + value

    def stripes(body):
        @pl.loop(0, width // stripe)
        def _(i):
            body(pl.ds(pl.multiple_of(i * stripe, stripe), stripe))

    hidden_ref[...] = gelu(dot(rows_ref[...], fc_ref[...]))
    stripes(lambda c: add(c, dot(hidden_ref[...], proj_ref[:, c]), True))

    for fc_a, fc_b, proj_a, proj_b in (
        (fc_up_ref, fc_up2_ref, proj_up_ref, proj_up2_ref),
        (fc_down_ref, fc_down2_ref, proj_down_ref, proj_down2_ref),
    ):
        def half(size, which):
            return pl.ds(pl.multiple_of(which * (size // 2), size // 2), size // 2)

        hidden_ref[...] = gelu(
            dot(rows_ref[:, half(width, core)], fc_a[...])
            + dot(rows_ref[:, half(width, 1 - core)], fc_b[...])
        )
        stripes(
            lambda c, proj_a=proj_a, proj_b=proj_b: add(
                c,
                dot(hidden_ref[:, half(units, core)], proj_a[:, c])
                + dot(hidden_ref[:, half(units, 1 - core)], proj_b[:, c]),
            )
        )

    begin = ring * head
    blocks = units // lanes
    fc = jnp.concatenate(
        [
            jnp.concatenate(
                [
                    gathered_ref[g, begin + b * lanes : begin + (b + 1) * lanes, :]
                    for b in range(blocks)
                ],
                axis=1,
            )
            for g in range(groups)
        ],
        axis=0,
    )
    hidden_ref[...] = gelu(dot(rows_ref[...], fc))
    begin = begin + units

    fold_lane = lax.broadcasted_iota(jnp.int32, (tokens // 2, lanes), 1)
    sides = ([], [])
    for i in range(0, ring, 2):
        a, b = heads_ref[i].astype(jnp.float32), heads_ref[i + 1].astype(jnp.float32)
        sides[0].append(jnp.where(fold_lane < head, a, pltpu.roll(b, head, 1)))
        sides[1].append(jnp.where(fold_lane < head, pltpu.roll(a, head, 1), b))
    attention = jnp.concatenate(
        [jnp.concatenate(side, axis=1) for side in sides], axis=0
    ).astype(jnp.bfloat16)

    per = stripe // lanes
    for i in range(groups // per):
        weights = [
            jnp.concatenate(
                [gathered_ref[i * per + g, rows, :] for g in range(per)], axis=1
            )
            for rows in (slice(begin, begin + units), slice(0, ring * head))
        ]
        columns = slice(i * stripe, (i + 1) * stripe)
        total = (
            total_ref[:, columns] + dot(hidden_ref[...], weights[0]) + dot(attention, weights[1])
        )
        total_ref[:, columns] = total
    for step in range(ring):
        source = pl.ds(pl.multiple_of(lax.rem(x + step, ring) * part, part), part)
        out_ref[step] = total_ref[source, :].astype(jnp.bfloat16)


def call(kernel, name, out_shape, smem, vmem, operands, scratch, limit, flops):
    specs = [pl.BlockSpec(memory_space=pltpu.SMEM)] * smem
    specs += [pl.BlockSpec(memory_space=pltpu.VMEM)] * vmem
    several = isinstance(out_shape, (tuple, list))
    spec = pl.BlockSpec(memory_space=pltpu.VMEM)
    return pl.pallas_call(
        kernel,
        out_shape=out_shape,
        in_specs=specs,
        out_specs=[spec] * len(out_shape) if several else spec,
        scratch_shapes=scratch,
        compiler_params=pltpu.CompilerParams(vmem_limit_bytes=limit * MIB),
        cost_estimate=pl.CostEstimate(flops=flops, bytes_accessed=4 * MIB, transcendentals=0),
        name=name,
    )(*operands)


def per_device(
    tokens, ln_gain, w_qkv, w_out, w_fc, w_proj, pool_kv, block_table, block_count, lengths
):
    bf16 = jnp.bfloat16
    ring = lax.axis_size("x")
    groups = lax.axis_size("z") * lax.axis_size("core")
    x, y = lax.axis_index("x"), lax.axis_index("y")
    core = lax.axis_index("core")
    group = lax.axis_index("z") * lax.axis_size("core") + core
    place = jnp.stack([x, y, core]).astype(jnp.int32)
    up = [(i, (i + 1) % ring) for i in range(ring)]
    down = [(i, (i - 1) % ring) for i in range(ring)]
    across = [(i, (i + 2) % ring) for i in range(ring)]
    swap = [(0, 1), (1, 0)]

    own = tokens[0]
    part, width = own.shape
    row_tok = part * ring
    group_tok = row_tok * ring
    local_pool = pool_kv[0]
    blk_dev, block_len, _, lanes = local_pool.shape
    pool_blocks = blk_dev * ring * ring
    head = lanes // 2
    units = w_fc.shape[1]
    slab = width // groups

    with jax.named_scope("small_weights"):
        small = jnp.concatenate([w_qkv[:, 0, :].T, w_out[0]], axis=0)
        slices = [
            small,
            lax.ppermute(small, "y", down),
            lax.ppermute(small, "y", across),
            lax.ppermute(small, "y", up),
        ]
        packed = jnp.concatenate(
            [s[head : 3 * head] for s in slices] + [s[:head] for s in slices], axis=0
        )
        qkv_weight = lax.all_gather(packed, ("z", "core"), axis=0, tiled=False)

    normed = layer_norm(own, ln_gain)
    with jax.named_scope("gather_tokens"):
        left = lax.ppermute(normed, "x", up)
        right = lax.ppermute(normed, "x", down)
        low = lax.ppermute(left[: part // 2], "x", up)
        high = lax.ppermute(right[part // 2 :], "x", down)

    with jax.named_scope("far_weights"):
        fc_slab = lax.dynamic_slice_in_dim(w_fc, group * slab, slab, 0)
        fc_slab = fc_slab.reshape(slab, units // lanes, lanes).transpose(1, 0, 2).reshape(-1, lanes)
        proj_slab = lax.dynamic_slice_in_dim(w_proj, group * slab, slab, 1)
        far = lax.ppermute(jnp.concatenate([fc_slab, proj_slab], axis=0), "y", across)
        outs = jnp.stack([s[3 * head :] for s in slices])
        outs = jnp.roll(outs, y, axis=0).reshape(ring * head, lanes)
        gathered = lax.all_gather(
            jnp.concatenate([outs, far], axis=0), ("z", "core"), axis=0, tiled=False
        )

    with jax.named_scope("near_weights"):
        fc_half = lax.dynamic_slice_in_dim(w_fc, core * (width // 2), width // 2, 0)
        proj_half = lax.dynamic_slice_in_dim(w_proj, core * (units // 2), units // 2, 0)
        near = []
        for way in (up, down):
            for half in (fc_half, proj_half):
                first = lax.ppermute(half, "y", way)
                near += [first, lax.ppermute(first, "core", swap)]

    pooled = lax.all_to_all(local_pool, ("y", "x"), split_axis=2, concat_axis=0, tiled=True)
    pooled = pooled.reshape(pool_blocks, block_len, lanes)

    cosine, sine = rotation_tables(
        lengths[0], block_count[0], y * row_tok, row_tok, block_len, lanes
    )
    payload = row_tok + row_tok // 2
    rows, sent = call(
        qkv_kernel, "qkv",
        (
            jax.ShapeDtypeStruct((row_tok, width), bf16),
            jax.ShapeDtypeStruct((ring, payload, lanes), bf16),
        ),
        1, 8, (place, normed, right, low, high, left, qkv_weight, cosine, sine),
        (), 40, 2 * row_tok * width * 3 * head * ring,
    )
    received = lax.all_to_all(sent, "y", split_axis=0, concat_axis=0, tiled=True)

    keys = block_table.shape[2] * block_len
    heads = call(
        functools.partial(attention_kernel, 512, 256, head**-0.5), "attend",
        jax.ShapeDtypeStruct((ring, row_tok // 2, lanes), bf16),
        3, 2, (block_table[0], block_count[0], lengths[0], received, pooled),
        [
            pltpu.VMEM((group_tok, lanes), bf16),
            pltpu.VMEM((group_tok, lanes), bf16),
            pltpu.VMEM((group_tok, lanes), bf16),
            pltpu.VMEM((keys, lanes), bf16),
            pltpu.VMEM((keys, lanes), bf16),
        ],
        24, 4 * group_tok * keys * lanes,
    )
    heads = lax.all_to_all(heads, "y", split_axis=0, concat_axis=0, tiled=True)

    partial = call(
        mix_kernel, "mix", jax.ShapeDtypeStruct((ring, part, width), bf16),
        1, 13, (place, rows, w_fc, w_proj, *near, gathered, heads),
        [pltpu.VMEM((row_tok, width), jnp.float32), pltpu.VMEM((row_tok, units), bf16)],
        48, 4 * row_tok * width * units * ring,
    )

    with jax.named_scope("reduce_tokens"):
        half = part // 2
        from_left = lax.ppermute(partial[2, :half], "x", up)
        from_right = lax.ppermute(partial[2, half:], "x", down)

        def plus(a, b):
            return (a.astype(jnp.float32) + b.astype(jnp.float32)).astype(bf16)

        to_right = jnp.concatenate([plus(partial[1, :half], from_left), partial[1, half:]], axis=0)
        to_left = jnp.concatenate([partial[3, :half], plus(partial[3, half:], from_right)], axis=0)
        a = lax.ppermute(to_right, "x", up).astype(jnp.float32)
        b = lax.ppermute(to_left, "x", down).astype(jnp.float32)
    summed = partial[0].astype(jnp.float32) + a + b
    return (own.astype(jnp.float32) + summed).astype(bf16)[None]


def solution(mesh):
    grid = Mesh(mesh.devices.reshape(8, 2, 4, 4), ("z", "core", "y", "x"))
    grp, pool = ("z", "core"), ("y", "x")
    in_specs = (
        P(grp, pool, None),
        P(),
        P(grp, pool, None),
        P(pool, None, grp),
        P(None, pool),
        P(pool, None),
        P(grp, pool, None, None, None),
        P(grp, None, None),
        P(grp, None),
        P(grp, None),
    )
    return jax.shard_map(
        per_device, mesh=grid, in_specs=in_specs, out_specs=P(grp, pool, None), check_vma=False
    )
```

```python
import functools

import jax
import jax.numpy as jnp
from jax import lax
from jax.experimental import pallas as pl
from jax.experimental.pallas import tpu as pltpu
from jax.sharding import Mesh
from jax.sharding import PartitionSpec as P

ROT = 32
LOG2E = 1.4426950408889634
MIB = 1024 * 1024
epsilon = 1e-05


def layer_norm(rows, gain):
    values = rows.astype(jnp.float32)
    centred = values - jnp.mean(values, axis=-1, keepdims=True)
    variance = jnp.mean(centred * centred, axis=-1, keepdims=True)
    return (centred * lax.rsqrt(variance + epsilon) * gain.astype(jnp.float32)).astype(jnp.bfloat16)


def rotation_tables(request_lengths, counts, first_token, tokens, block_len, lanes):
    half = ROT // 2
    ends = jnp.cumsum(request_lengths)
    starts = ends - request_lengths
    index = first_token + jnp.arange(tokens, dtype=jnp.int32)
    inside = (index[:, None] >= starts[None, :]) & (index[:, None] < ends[None, :])
    position = (
        jnp.sum(jnp.where(inside, (counts * block_len - starts)[None, :], 0), axis=-1) + index
    )
    frequency = 10000.0 ** (-2.0 * jnp.arange(half, dtype=jnp.float32) / ROT)
    lane = jnp.arange(lanes, dtype=jnp.int32)
    spread = jnp.where(lane < ROT, jnp.tile(frequency, lanes // half), 0.0)
    angle = position.astype(jnp.float32)[:, None] * spread[None, :]
    sine = jnp.sin(angle)
    return jnp.cos(angle), jnp.where(lane[None, :] < half, -sine, sine)


def qkv_kernel(
    ring, place_ref, cosine_ref, sine_ref, own_ref, right_ref, opposite_ref, left_ref,
    gathered_ref, rows_ref, *refs
):
    sent_refs, (weight_ref, cos_ref, sin_ref, sems) = refs[:ring], refs[ring:]
    x = place_ref[0]
    part = own_ref.shape[0]
    tokens, lanes = cos_ref.shape
    head = lanes // 2

    copies = [
        pltpu.make_async_copy(source, target, sems.at[k])
        for k, (source, target) in enumerate(
            ((gathered_ref, weight_ref), (cosine_ref, cos_ref), (sine_ref, sin_ref))
        )
    ]
    for step, piece in enumerate((own_ref, right_ref, opposite_ref, left_ref)):
        begin = pl.multiple_of(lax.rem(x + step, ring) * part, part)
        target = rows_ref.at[pl.ds(begin, part), :]
        copies.append(pltpu.make_async_copy(piece, target, sems.at[len(copies)]))
    for copy in copies:
        copy.start()
    for copy in copies:
        copy.wait()
    lane = lax.broadcasted_iota(jnp.int32, (tokens, lanes), 1)

    def rotated(field):
        other = jnp.where(
            lane < ROT // 2, pltpu.roll(field, lanes - ROT // 2, 1), pltpu.roll(field, ROT // 2, 1)
        )
        return field * cos_ref[...] + other * sin_ref[...]

    def product(begin, size):
        weight = jnp.concatenate(
            [weight_ref[g, begin : begin + size, :] for g in range(weight_ref.shape[0])], axis=1
        )
        return lax.dot_general(
            rows_ref[...], weight, (((1,), (1,)), ((), ())), preferred_element_type=jnp.float32
        )

    for pair in range(ring // 2):
        both = product(pair * 2 * lanes, 2 * lanes)
        for k in range(2):
            field = rotated(both[:, k * lanes : (k + 1) * lanes])
            sent_refs[2 * pair + k][:tokens, :] = field.astype(jnp.bfloat16)
    queries = product(ring * lanes, ring * head)
    for d in range(ring):
        field = queries[:, d // 2 * lanes : (d // 2 + 1) * lanes]
        if d % 2:
            field = pltpu.roll(field, head, 1)
        field = rotated(field)
        top, bottom = field[: tokens // 2], pltpu.roll(field[tokens // 2 :], head, 1)
        folded = jnp.where(lane[: tokens // 2] < head, top, bottom)
        sent_refs[d][tokens:, :] = folded.astype(jnp.bfloat16)


def attention_kernel(
    chunk, tile, scale, ring, place_ref, table_ref, count_ref, length_ref, pool_ref, *refs
):
    sent_refs, out_refs = refs[:ring], refs[ring : 2 * ring]
    query_ref, fresh_ref, worth_ref, result_ref, key_ref, value_ref, score_ref = refs[2 * ring :]
    y = place_ref[1]
    tokens, lanes = query_ref.shape
    head = lanes // 2
    part = tokens // ring
    block_len = pool_ref.shape[1]
    requests = table_ref.shape[0]
    per_chunk = chunk // block_len
    factor = scale * LOG2E
    unroll = 8
    block_lane = lax.broadcasted_iota(jnp.int32, (block_len, lanes), 1)
    fold_lane = lax.broadcasted_iota(jnp.int32, (part // 2, lanes), 1)
    part_lane = lax.broadcasted_iota(jnp.int32, (part, lanes), 1)
    one = jnp.ones((), jnp.bfloat16)
    nil = jnp.zeros((), jnp.bfloat16)

    fresh_ref[tokens:, :] = jnp.zeros((fresh_ref.shape[0] - tokens, lanes), jnp.bfloat16)
    worth_ref[tokens:, :] = jnp.zeros((fresh_ref.shape[0] - tokens, lanes), jnp.bfloat16)
    for i in range(ring):
        both = sent_refs[i][:part, :]
        origin = lax.rem(y + ring - i, ring) * part
        block = pl.ds(pl.multiple_of(origin, part), part)
        fresh_ref[block, :] = both
        worth_ref[block, :] = jnp.where(part_lane < head, one, both)
        folded = sent_refs[i][part:, :].astype(jnp.float32)
        for k in range(2):
            unfolded = folded if k == 0 else pltpu.roll(folded, head, 1)
            begin = pl.multiple_of(origin + k * (part // 2), part // 2)
            query_ref[pl.ds(begin, part // 2), :] = jnp.where(
                fold_lane < head, unfolded, 0.0
            ).astype(jnp.bfloat16)

    def dot_t(a, b):
        return lax.dot_general(a, b, (((1,), (1,)), ((), ())), preferred_element_type=jnp.float32)

    def peak(highest, scores):
        for k in range(chunk // lanes):
            highest = jnp.maximum(highest, scores[:, k * lanes : (k + 1) * lanes])
        return highest

    def request(r, start):
        length = length_ref[r]
        count = count_ref[r]
        chunks = (count + per_chunk - 1) // per_chunk

        def gather(i, _):
            for u in range(unroll):
                b = i * unroll + u
                block = pool_ref[table_ref[r, jnp.minimum(b, count - 1)]]
                where = pl.ds(pl.multiple_of(b * block_len, block_len), block_len)
                key_ref[where, :] = block
                paired = jnp.where(block_lane < head, one, block)
                value_ref[where, :] = jnp.where(b < count, paired, nil)
            return 0

        lax.fori_loop(0, chunks * (per_chunk // unroll), gather, 0)
        first = start // 16 * 16
        tiles = (start + length - first + tile - 1) // tile

        def one_tile(i, _):
            row = pl.multiple_of(jnp.minimum(first + i * tile, tokens - tile), 16)
            rows = pl.ds(row, tile)
            query = query_ref[rows, :]
            fresh_chunks = (row + tile - first + chunk - 1) // chunk
            own = row + lax.broadcasted_iota(jnp.int32, (tile, chunk), 0)
            column = first + lax.broadcasted_iota(jnp.int32, (tile, chunk), 1)

            def at(j):
                return pl.ds(pl.multiple_of(j * chunk, chunk), chunk)

            def fresh_at(j):
                return pl.ds(pl.multiple_of(first + j * chunk, 16), chunk)

            def look(j, highest):
                scores = dot_t(query, key_ref[at(j), :])
                score_ref[:, at(j)] = scores
                return peak(highest, scores)

            def look_fresh(j, highest):
                scores = dot_t(query, fresh_ref[fresh_at(j), :])
                other = column + j * chunk
                visible = (other >= start) & (other <= own)
                scores = jnp.where(visible, scores, -1e30)
                score_ref[:, at(chunks + j)] = scores
                return peak(highest, scores)

            highest = jnp.full((tile, lanes), -1e30, jnp.float32)
            highest = lax.fori_loop(0, chunks, look, highest)
            highest = lax.fori_loop(0, fresh_chunks, look_fresh, highest)
            top = factor * jnp.max(highest, axis=-1, keepdims=True)

            def weigh(j, acc):
                weights = jnp.exp2(factor * score_ref[:, at(j)] - top).astype(jnp.bfloat16)
                return acc + jnp.dot(
                    weights, value_ref[at(j), :], preferred_element_type=jnp.float32
                )

            def weigh_fresh(j, acc):
                weights = jnp.exp2(factor * score_ref[:, at(chunks + j)] - top).astype(jnp.bfloat16)
                return acc + jnp.dot(
                    weights, worth_ref[fresh_at(j), :], preferred_element_type=jnp.float32
                )

            acc = jnp.zeros((tile, lanes), jnp.float32)
            acc = lax.fori_loop(0, chunks, weigh, acc)
            acc = lax.fori_loop(0, fresh_chunks, weigh_fresh, acc)
            result = (acc / pltpu.roll(acc, head, 1)).astype(jnp.bfloat16)
            place = row + lax.broadcasted_iota(jnp.int32, (tile, lanes), 0)
            inside = (place >= start) & (place < start + length)
            result_ref[rows, :] = jnp.where(inside, result, result_ref[rows, :])
            return 0

        lax.fori_loop(0, tiles, one_tile, 0)
        return start + length

    lax.fori_loop(0, requests, request, 0)
    for i in range(ring):
        begin = pl.multiple_of(lax.rem(y + i, ring) * part, part)
        top = result_ref[pl.ds(begin, part // 2), :].astype(jnp.float32)
        bottom = result_ref[pl.ds(begin + part // 2, part // 2), :].astype(jnp.float32)
        out_refs[i][...] = jnp.where(fold_lane < head, pltpu.roll(top, head, 1), bottom).astype(
            jnp.bfloat16
        )


def gelu(value):
    return jax.nn.gelu(value, approximate=True).astype(jnp.bfloat16)


def dot(a, b):
    return jnp.dot(a, b, preferred_element_type=jnp.float32)


def hide_kernel(rows_ref, *refs):
    half = len(refs) // 2
    for fc_ref, hidden_ref in zip(refs[:half], refs[half:]):
        hidden_ref[...] = gelu(dot(rows_ref[...], fc_ref[...]))


def mix_kernel(
    steps, hide, place_ref, own_ref, near_ref, other_ref,
    head0_ref, head1_ref, head2_ref, head3_ref,
    given_ref, proj_own_hbm, proj_near_hbm, proj_other_hbm, gathered_ref, *refs
):
    out_refs, refs = refs[:-7], refs[-7:]
    attention_ref, held_ref, far_ref, proj_own_ref, proj_near_ref, proj_other_ref, sems = refs
    x = place_ref[0]
    tokens, units = own_ref.shape
    width = proj_own_ref.shape[1]
    groups, held, lanes = gathered_ref.shape
    begin = held - 2 * units
    head = lanes // 2
    ring = attention_ref.shape[1] // head
    part = tokens // ring
    stripe = 512

    moves = [(given_ref, far_ref)]
    for rows in [pl.ds(begin, units)] * hide + [pl.ds(held - units, units), pl.ds(0, begin)]:
        moves.append((gathered_ref.at[:, rows, :], held_ref.at[:, rows, :]))
    moves += [
        (proj_own_hbm, proj_own_ref), (proj_near_hbm, proj_near_ref),
        (proj_other_hbm, proj_other_ref),
    ]
    copies = [
        pltpu.make_async_copy(source, target, sems.at[k])
        for k, (source, target) in enumerate(moves)
    ]
    for copy in copies:
        copy.start()
    fold_lane = lax.broadcasted_iota(jnp.int32, (tokens // 2, lanes), 1)
    for k, (first, second) in enumerate(((head0_ref, head1_ref), (head2_ref, head3_ref))):
        a, b = first[...].astype(jnp.float32), second[...].astype(jnp.float32)
        columns = slice(k * lanes, (k + 1) * lanes)
        attention_ref[: tokens // 2, columns] = jnp.where(
            fold_lane < head, a, pltpu.roll(b, head, 1)
        ).astype(jnp.bfloat16)
        attention_ref[tokens // 2 :, columns] = jnp.where(
            fold_lane < head, pltpu.roll(a, head, 1), b
        ).astype(jnp.bfloat16)

    def take(ref):
        return jnp.concatenate(
            [
                ref[pl.ds(pl.multiple_of(lax.rem(x + step, ring) * part, part), part), :]
                for step in steps
            ],
            axis=0,
        )

    if hide:
        for copy in copies[:2]:
            copy.wait()
        fc = jnp.concatenate(
            [
                jnp.concatenate(
                    [
                        held_ref[g, begin + b * lanes : begin + (b + 1) * lanes, :]
                        for b in range(units // lanes)
                    ],
                    axis=1,
                )
                for g in range(groups)
            ],
            axis=0,
        )
        out_refs[-1][...] = gelu(dot(far_ref[...], fc))
        far_ref, out_refs = out_refs[-1], out_refs[:-1]
    for copy in copies[2 * hide :]:
        copy.wait()
    values = [take(ref) for ref in (own_ref, near_ref, other_ref, far_ref, attention_ref)]
    per = stripe // lanes
    for i in range(width // stripe):
        columns = slice(i * stripe, (i + 1) * stripe)
        weights = [ref[:, columns] for ref in (proj_own_ref, proj_near_ref, proj_other_ref)]
        for rows in (slice(held - units, held), slice(0, ring * head)):
            weights.append(
                jnp.concatenate([held_ref[i * per + g, rows, :] for g in range(per)], axis=1)
            )
        total = dot(values[0], weights[0])
        for value, weight in zip(values[1:], weights[1:]):
            total += dot(value, weight)
        total = total.astype(jnp.bfloat16)
        row = 0
        for out_ref in out_refs:
            size = out_ref.shape[0]
            out_ref[:, columns] = total[row : row + size]
            row += size


def call(kernel, name, out_shape, smem, vmem, operands, scratch, limit, flops, anywhere=0):
    specs = [pl.BlockSpec(memory_space=pltpu.SMEM)] * smem
    specs += [pl.BlockSpec(memory_space=pltpu.VMEM)] * vmem
    specs += [pl.BlockSpec(memory_space=pltpu.HBM)] * anywhere
    several = isinstance(out_shape, (tuple, list))
    spec = pl.BlockSpec(memory_space=pltpu.VMEM)
    return pl.pallas_call(
        kernel,
        out_shape=out_shape,
        in_specs=specs,
        out_specs=[spec] * len(out_shape) if several else spec,
        scratch_shapes=scratch,
        compiler_params=pltpu.CompilerParams(vmem_limit_bytes=limit * MIB),
        cost_estimate=pl.CostEstimate(flops=flops, bytes_accessed=4 * MIB, transcendentals=0),
        name=name,
    )(*operands)


def per_device(
    tokens, ln_gain, w_qkv, w_out, w_fc, w_proj, pool_kv, block_table, block_count, lengths
):
    bf16 = jnp.bfloat16
    ring = lax.axis_size("x")
    groups = lax.axis_size("z") * lax.axis_size("core")
    x, y = lax.axis_index("x"), lax.axis_index("y")
    core = lax.axis_index("core")
    group = lax.axis_index("z") * lax.axis_size("core") + core
    place = jnp.stack([x, y, core]).astype(jnp.int32)
    up = [(i, (i + 1) % ring) for i in range(ring)]
    down = [(i, (i - 1) % ring) for i in range(ring)]
    across = [(i, (i + 2) % ring) for i in range(ring)]
    swap = [(0, 1), (1, 0)]

    own = tokens[0]
    part, width = own.shape
    row_tok = part * ring
    group_tok = row_tok * ring
    local_pool = pool_kv[0]
    blk_dev, block_len, _, lanes = local_pool.shape
    pool_blocks = blk_dev * ring * ring
    head = lanes // 2
    units = w_fc.shape[1]
    slab = width // groups

    with jax.named_scope("small_weights"):
        small = jnp.concatenate([w_qkv[:, 0, :].T, w_out[0]], axis=0)
        slices = [
            small,
            lax.ppermute(small, "y", down),
            lax.ppermute(small, "y", across),
            lax.ppermute(small, "y", up),
        ]
        packed = jnp.concatenate(
            [s[head : 3 * head] for s in slices] + [s[:head] for s in slices], axis=0
        )
        qkv_weight = lax.all_gather(packed, ("z", "core"), axis=0, tiled=False)

    normed = layer_norm(own, ln_gain)
    fan = [(i, (i + 1) % ring) for i in range(ring)]
    fan += [(ring + i, ring + (i - 1) % ring) for i in range(ring)]
    with jax.named_scope("gather_tokens"):
        left = lax.ppermute(normed, "x", up)
        right = lax.ppermute(normed, "x", down)
        opposite = lax.ppermute(jnp.where(core == 0, left, right), ("core", "x"), fan)

    def after(value, other):
        return lax.optimization_barrier((value, other))[0]

    with jax.named_scope("far_weights"):
        fc_slab = lax.dynamic_slice_in_dim(after(w_fc, normed), group * slab, slab, 0)
        pieces = [fc_slab[:, b : b + lanes] for b in range(0, units, lanes)]
        proj_slab = lax.dynamic_slice_in_dim(after(w_proj, normed), group * slab, slab, 1)
        payload = jnp.concatenate(pieces + [proj_slab], axis=0)
        far = lax.ppermute(payload, "y", across)

    with jax.named_scope("near_weights"):
        fc_near = lax.ppermute(after(w_fc, payload), ("core", "y"), fan)

    pooled = lax.all_to_all(
        after(local_pool, left), ("y", "x"), split_axis=2, concat_axis=0, tiled=True
    )
    pooled = pooled.reshape(pool_blocks, block_len, lanes)
    cosine, sine = rotation_tables(
        lengths[0], block_count[0], y * row_tok, row_tok, block_len, lanes
    )
    payload = row_tok + row_tok // 2
    sent_shape = jax.ShapeDtypeStruct((payload, lanes), bf16)
    rows, *sent = call(
        functools.partial(qkv_kernel, ring), "qkv",
        [jax.ShapeDtypeStruct((row_tok, width), bf16)] + [sent_shape] * ring,
        1, 0, (place, cosine, sine, normed, right, opposite, left, qkv_weight),
        [
            pltpu.VMEM((groups, 3 * head * ring, lanes), bf16),
            pltpu.VMEM((row_tok, lanes), jnp.float32),
            pltpu.VMEM((row_tok, lanes), jnp.float32),
            pltpu.SemaphoreType.DMA((7,)),
        ],
        56, 3_000 * MIB, 7,
    )
    gathered = lax.all_gather(
        after(jnp.concatenate([s[3 * head :] for s in slices] + [far], axis=0), (rows, pooled, fc_near)),
        ("z", "core"), axis=0, tiled=False,
    )
    ways = (None, up, across, down)

    def exchange(pieces):
        return [pieces[0]] + [lax.ppermute(p, "y", w) for p, w in zip(pieces[1:], ways[1:])]

    received = exchange(sent)
    work = 2 * row_tok * width * units
    hidden_shape = jax.ShapeDtypeStruct((row_tok, units), bf16)
    work = 2 * row_tok * width * units
    fc_other = lax.ppermute(fc_near, "core", swap)
    own_hidden, near_hidden = call(
        hide_kernel, "hide", [hidden_shape] * 2, 0, 3, (rows, w_fc, fc_near), (), 8, 2 * work
    )
    (other_hidden,) = call(
        hide_kernel, "hide", [hidden_shape], 0, 2, (rows, fc_other), (), 8, work
    )
    proj_near = lax.ppermute(after(w_proj, tuple(received[1:])), ("core", "y"), fan)

    keys = block_table.shape[2] * block_len
    chunk, tile = 512, 256
    most = -(-(group_tok // 4 + tile + 16) // chunk) * chunk
    heads = call(
        functools.partial(attention_kernel, chunk, tile, head**-0.5, ring), "attend",
        [jax.ShapeDtypeStruct((row_tok // 2, lanes), bf16)] * ring,
        4, 1 + ring, (after(place, (own_hidden, near_hidden, other_hidden)), block_table[0], block_count[0], lengths[0], pooled, *received),
        [
            pltpu.VMEM((group_tok, lanes), bf16),
            pltpu.VMEM((group_tok + most, lanes), bf16),
            pltpu.VMEM((group_tok + most, lanes), bf16),
            pltpu.VMEM((group_tok, lanes), bf16),
            pltpu.VMEM((keys, lanes), bf16),
            pltpu.VMEM((keys, lanes), bf16),
            pltpu.VMEM((tile, keys + most), jnp.float32),
        ],
        12, 30_000 * MIB,
    )
    proj_other = lax.ppermute(after(proj_near, heads[0]), "core", swap)
    heads = exchange(heads)
    block_shape = jax.ShapeDtypeStruct((part, width), bf16)

    def mix(steps, shapes, given, hide):
        return call(
            functools.partial(mix_kernel, steps, hide), "mix", shapes, 1, 7,
            (
                place, own_hidden, near_hidden, other_hidden,
                heads[0], heads[3], heads[2], heads[1],
                given, w_proj, proj_near, proj_other, gathered,
            ),
            [
                pltpu.VMEM((row_tok, ring * head), bf16),
                pltpu.VMEM(gathered.shape, bf16),
                pltpu.VMEM(given.shape, bf16),
                pltpu.VMEM(w_proj.shape, bf16),
                pltpu.VMEM(w_proj.shape, bf16),
                pltpu.VMEM(w_proj.shape, bf16),
                pltpu.SemaphoreType.DMA((7,)),
            ],
            52, (len(steps) + 2 * hide) * work, 5,
        )

    out2, far_hidden = mix((2,), [block_shape, hidden_shape], rows, True)
    out1, out3, out0 = mix((1, 3, 0), [block_shape] * 3, far_hidden, False)

    with jax.named_scope("reduce_tokens"):
        passed = lax.ppermute(out2, ("core", "x"), fan).astype(jnp.float32)

        def joined(block, which):
            added = jnp.where(core == which, passed, 0.0)
            return (block.astype(jnp.float32) + added).astype(bf16)

        a = lax.ppermute(joined(out1, 0), "x", up).astype(jnp.float32)
        b = lax.ppermute(joined(out3, 1), "x", down).astype(jnp.float32)
    summed = out0.astype(jnp.float32) + a + b
    return (own.astype(jnp.float32) + summed).astype(bf16)[None]


def solution(mesh):
    grid = Mesh(mesh.devices.reshape(8, 2, 4, 4), ("z", "core", "y", "x"))
    grp, pool = ("z", "core"), ("y", "x")
    in_specs = (
        P(grp, pool, None),
        P(),
        P(grp, pool, None),
        P(pool, None, grp),
        P(None, pool),
        P(pool, None),
        P(grp, pool, None, None, None),
        P(grp, None, None),
        P(grp, None),
        P(grp, None),
    )
    return jax.shard_map(
        per_device, mesh=grid, in_specs=in_specs, out_specs=P(grp, pool, None), check_vma=False
    )
```

```python
import functools

import jax
import jax.numpy as jnp
from jax import lax
from jax.experimental import pallas as pl
from jax.experimental.pallas import tpu as pltpu
from jax.sharding import Mesh
from jax.sharding import PartitionSpec as P

ROT = 32
LOG2E = 1.4426950408889634
MIB = 1024 * 1024
epsilon = 1e-05


def layer_norm(rows, gain):
    values = rows.astype(jnp.float32)
    centred = values - jnp.mean(values, axis=-1, keepdims=True)
    variance = jnp.mean(centred * centred, axis=-1, keepdims=True)
    return (centred * lax.rsqrt(variance + epsilon) * gain.astype(jnp.float32)).astype(jnp.bfloat16)


def rotation_tables(request_lengths, counts, first_token, tokens, block_len, lanes):
    half = ROT // 2
    ends = jnp.cumsum(request_lengths)
    starts = ends - request_lengths
    index = first_token + jnp.arange(tokens, dtype=jnp.int32)
    inside = (index[:, None] >= starts[None, :]) & (index[:, None] < ends[None, :])
    position = (
        jnp.sum(jnp.where(inside, (counts * block_len - starts)[None, :], 0), axis=-1) + index
    )
    frequency = 10000.0 ** (-2.0 * jnp.arange(half, dtype=jnp.float32) / ROT)
    lane = jnp.arange(lanes, dtype=jnp.int32)
    spread = jnp.where(lane < ROT, jnp.tile(frequency, lanes // half), 0.0)
    angle = position.astype(jnp.float32)[:, None] * spread[None, :]
    sine = jnp.sin(angle)
    return jnp.cos(angle), jnp.where(lane[None, :] < half, -sine, sine)


def qkv_kernel(
    ring, place_ref, cosine_ref, sine_ref, own_ref, right_ref, opposite_ref, left_ref,
    gathered_ref, rows_ref, *refs
):
    sent_refs, (weight_ref, cos_ref, sin_ref, sems) = refs[:ring], refs[ring:]
    x = place_ref[0]
    part = own_ref.shape[0]
    tokens, lanes = cos_ref.shape
    head = lanes // 2

    copies = [
        pltpu.make_async_copy(source, target, sems.at[k])
        for k, (source, target) in enumerate(
            ((gathered_ref, weight_ref), (cosine_ref, cos_ref), (sine_ref, sin_ref))
        )
    ]
    for step, piece in enumerate((own_ref, right_ref, opposite_ref, left_ref)):
        begin = pl.multiple_of(lax.rem(x + step, ring) * part, part)
        target = rows_ref.at[pl.ds(begin, part), :]
        copies.append(pltpu.make_async_copy(piece, target, sems.at[len(copies)]))
    for copy in copies:
        copy.start()
    for copy in copies:
        copy.wait()
    lane = lax.broadcasted_iota(jnp.int32, (tokens, lanes), 1)

    def rotated(field):
        other = jnp.where(
            lane < ROT // 2, pltpu.roll(field, lanes - ROT // 2, 1), pltpu.roll(field, ROT // 2, 1)
        )
        return field * cos_ref[...] + other * sin_ref[...]

    def product(begin, size):
        weight = jnp.concatenate(
            [weight_ref[g, begin : begin + size, :] for g in range(weight_ref.shape[0])], axis=1
        )
        return lax.dot_general(
            rows_ref[...], weight, (((1,), (1,)), ((), ())), preferred_element_type=jnp.float32
        )

    for pair in range(ring // 2):
        both = product(pair * 2 * lanes, 2 * lanes)
        for k in range(2):
            field = rotated(both[:, k * lanes : (k + 1) * lanes])
            sent_refs[2 * pair + k][:tokens, :] = field.astype(jnp.bfloat16)
    queries = product(ring * lanes, ring * head)
    for d in range(ring):
        field = queries[:, d // 2 * lanes : (d // 2 + 1) * lanes]
        if d % 2:
            field = pltpu.roll(field, head, 1)
        field = rotated(field)
        top, bottom = field[: tokens // 2], pltpu.roll(field[tokens // 2 :], head, 1)
        folded = jnp.where(lane[: tokens // 2] < head, top, bottom)
        sent_refs[d][tokens:, :] = folded.astype(jnp.bfloat16)


def attention_kernel(
    chunk, tile, scale, ring, place_ref, table_ref, count_ref, length_ref, pool_ref, *refs
):
    sent_refs, out_refs = refs[:ring], refs[ring : 2 * ring]
    query_ref, fresh_ref, worth_ref, result_ref, key_ref, value_ref, score_ref = refs[2 * ring :]
    y = place_ref[1]
    tokens, lanes = query_ref.shape
    head = lanes // 2
    part = tokens // ring
    block_len = pool_ref.shape[1]
    requests = table_ref.shape[0]
    per_chunk = chunk // block_len
    factor = scale * LOG2E
    unroll = 8
    block_lane = lax.broadcasted_iota(jnp.int32, (block_len, lanes), 1)
    fold_lane = lax.broadcasted_iota(jnp.int32, (part // 2, lanes), 1)
    part_lane = lax.broadcasted_iota(jnp.int32, (part, lanes), 1)
    one = jnp.ones((), jnp.bfloat16)
    nil = jnp.zeros((), jnp.bfloat16)

    fresh_ref[tokens:, :] = jnp.zeros((fresh_ref.shape[0] - tokens, lanes), jnp.bfloat16)
    worth_ref[tokens:, :] = jnp.zeros((fresh_ref.shape[0] - tokens, lanes), jnp.bfloat16)
    for i in range(ring):
        both = sent_refs[i][:part, :]
        origin = lax.rem(y + ring - i, ring) * part
        block = pl.ds(pl.multiple_of(origin, part), part)
        fresh_ref[block, :] = both
        worth_ref[block, :] = jnp.where(part_lane < head, one, both)
        folded = sent_refs[i][part:, :].astype(jnp.float32)
        for k in range(2):
            unfolded = folded if k == 0 else pltpu.roll(folded, head, 1)
            begin = pl.multiple_of(origin + k * (part // 2), part // 2)
            query_ref[pl.ds(begin, part // 2), :] = jnp.where(
                fold_lane < head, unfolded, 0.0
            ).astype(jnp.bfloat16)

    def dot_t(a, b):
        return lax.dot_general(a, b, (((1,), (1,)), ((), ())), preferred_element_type=jnp.float32)

    def peak(highest, scores):
        for k in range(0, scores.shape[1], lanes):
            highest = jnp.maximum(highest, scores[:, k : k + lanes])
        return highest

    def request(r, start):
        length = length_ref[r]
        count = count_ref[r]
        chunks = (count + per_chunk - 1) // per_chunk
        pairs = chunks // 2

        def gather(i, _):
            for u in range(unroll):
                b = i * unroll + u
                block = pool_ref[table_ref[r, jnp.minimum(b, count - 1)]]
                where = pl.ds(pl.multiple_of(b * block_len, block_len), block_len)
                key_ref[where, :] = block
                paired = jnp.where(block_lane < head, one, block)
                value_ref[where, :] = jnp.where(b < count, paired, nil)
            return 0

        lax.fori_loop(0, chunks * (per_chunk // unroll), gather, 0)
        first = start // 16 * 16
        tiles = (start + length - first + tile - 1) // tile

        def one_tile(i, _):
            row = pl.multiple_of(jnp.minimum(first + i * tile, tokens - tile), 16)
            rows = pl.ds(row, tile)
            query = query_ref[rows, :]
            fresh_chunks = (row + tile - first + chunk - 1) // chunk
            own = row + lax.broadcasted_iota(jnp.int32, (tile, chunk), 0)
            column = first + lax.broadcasted_iota(jnp.int32, (tile, chunk), 1)

            def at(j):
                return pl.ds(pl.multiple_of(j * chunk, chunk), chunk)

            def fresh_at(j):
                return pl.ds(pl.multiple_of(first + j * chunk, 16), chunk)

            def look(size):
                def body(j, highest):
                    where = pl.ds(pl.multiple_of(j * size, size), size)
                    scores = dot_t(query, key_ref[where, :])
                    score_ref[:, where] = scores
                    return peak(highest, scores)

                return body

            def look_fresh(j, highest):
                scores = dot_t(query, fresh_ref[fresh_at(j), :])
                other = column + j * chunk
                visible = (other >= start) & (other <= own)
                scores = jnp.where(visible, scores, -1e30)
                score_ref[:, at(chunks + j)] = scores
                return peak(highest, scores)

            highest = jnp.full((tile, lanes), -1e30, jnp.float32)
            highest = lax.fori_loop(0, pairs, look(2 * chunk), highest)
            highest = lax.fori_loop(2 * pairs, chunks, look(chunk), highest)
            highest = lax.fori_loop(0, fresh_chunks, look_fresh, highest)
            top = factor * jnp.max(highest, axis=-1, keepdims=True)

            def weigh(size):
                def body(j, acc):
                    where = pl.ds(pl.multiple_of(j * size, size), size)
                    weights = jnp.exp2(factor * score_ref[:, where] - top).astype(jnp.bfloat16)
                    return acc + dot(weights, value_ref[where, :])

                return body

            def weigh_fresh(j, acc):
                weights = jnp.exp2(factor * score_ref[:, at(chunks + j)] - top).astype(jnp.bfloat16)
                return acc + jnp.dot(
                    weights, worth_ref[fresh_at(j), :], preferred_element_type=jnp.float32
                )

            acc = jnp.zeros((tile, lanes), jnp.float32)
            acc = lax.fori_loop(0, pairs, weigh(2 * chunk), acc)
            acc = lax.fori_loop(2 * pairs, chunks, weigh(chunk), acc)
            acc = lax.fori_loop(0, fresh_chunks, weigh_fresh, acc)
            result = (acc / pltpu.roll(acc, head, 1)).astype(jnp.bfloat16)
            place = row + lax.broadcasted_iota(jnp.int32, (tile, lanes), 0)
            inside = (place >= start) & (place < start + length)
            result_ref[rows, :] = jnp.where(inside, result, result_ref[rows, :])
            return 0

        lax.fori_loop(0, tiles, one_tile, 0)
        return start + length

    lax.fori_loop(0, requests, request, 0)
    for i in range(ring):
        begin = pl.multiple_of(lax.rem(y + i, ring) * part, part)
        top = result_ref[pl.ds(begin, part // 2), :].astype(jnp.float32)
        bottom = result_ref[pl.ds(begin + part // 2, part // 2), :].astype(jnp.float32)
        out_refs[i][...] = jnp.where(fold_lane < head, pltpu.roll(top, head, 1), bottom).astype(
            jnp.bfloat16
        )


def gelu(value):
    return jax.nn.gelu(value, approximate=True).astype(jnp.bfloat16)


def dot(a, b):
    return jnp.dot(a, b, preferred_element_type=jnp.float32)


def hide_kernel(rows_ref, *refs):
    half = len(refs) // 2
    for fc_ref, hidden_ref in zip(refs[:half], refs[half:]):
        hidden_ref[...] = gelu(dot(rows_ref[...], fc_ref[...]))


def mix_kernel(
    steps, hide, place_ref, own_ref, near_ref, other_ref,
    head0_ref, head1_ref, head2_ref, head3_ref,
    given_ref, proj_own_hbm, proj_near_hbm, proj_other_hbm, gathered_ref, *refs
):
    out_refs, refs = refs[:-7], refs[-7:]
    attention_ref, held_ref, far_ref, proj_own_ref, proj_near_ref, proj_other_ref, sems = refs
    x = place_ref[0]
    tokens, units = own_ref.shape
    width = proj_own_ref.shape[1]
    groups, held, lanes = gathered_ref.shape
    begin = held - 2 * units
    head = lanes // 2
    ring = attention_ref.shape[1] // head
    part = tokens // ring
    stripe = 512

    per = stripe // lanes
    moves = [(given_ref, far_ref)]
    if hide:
        moves.append(
            (gathered_ref.at[:, pl.ds(begin, units), :], held_ref.at[:, pl.ds(begin, units), :])
        )
    ready = len(moves)
    for i in range(width // stripe):
        columns, share = pl.ds(i * stripe, stripe), pl.ds(i * per, per)
        for source, target in (
            (proj_own_hbm, proj_own_ref), (proj_near_hbm, proj_near_ref),
            (proj_other_hbm, proj_other_ref),
        ):
            moves.append((source.at[:, columns], target.at[:, columns]))
        for rows in (pl.ds(held - units, units), pl.ds(0, begin)):
            moves.append((gathered_ref.at[share, rows, :], held_ref.at[share, rows, :]))
    copies = [
        pltpu.make_async_copy(source, target, sems.at[k])
        for k, (source, target) in enumerate(moves)
    ]
    for copy in copies:
        copy.start()
    fold_lane = lax.broadcasted_iota(jnp.int32, (tokens // 2, lanes), 1)
    for k, (first, second) in enumerate(((head0_ref, head1_ref), (head2_ref, head3_ref))):
        a, b = first[...].astype(jnp.float32), second[...].astype(jnp.float32)
        columns = slice(k * lanes, (k + 1) * lanes)
        attention_ref[: tokens // 2, columns] = jnp.where(
            fold_lane < head, a, pltpu.roll(b, head, 1)
        ).astype(jnp.bfloat16)
        attention_ref[tokens // 2 :, columns] = jnp.where(
            fold_lane < head, pltpu.roll(a, head, 1), b
        ).astype(jnp.bfloat16)

    def take(ref):
        return jnp.concatenate(
            [
                ref[pl.ds(pl.multiple_of(lax.rem(x + step, ring) * part, part), part), :]
                for step in steps
            ],
            axis=0,
        )

    for copy in copies[:ready]:
        copy.wait()
    if hide:
        fc = jnp.concatenate(
            [
                jnp.concatenate(
                    [
                        held_ref[g, begin + b * lanes : begin + (b + 1) * lanes, :]
                        for b in range(units // lanes)
                    ],
                    axis=1,
                )
                for g in range(groups)
            ],
            axis=0,
        )
        out_refs[-1][...] = gelu(dot(far_ref[...], fc))
        far_ref, out_refs = out_refs[-1], out_refs[:-1]
    values = [take(ref) for ref in (own_ref, near_ref, other_ref, far_ref, attention_ref)]
    for i in range(width // stripe):
        for copy in copies[ready + 5 * i : ready + 5 * (i + 1)]:
            copy.wait()
        columns = slice(i * stripe, (i + 1) * stripe)
        weights = [ref[:, columns] for ref in (proj_own_ref, proj_near_ref, proj_other_ref)]
        for rows in (slice(held - units, held), slice(0, ring * head)):
            weights.append(
                jnp.concatenate([held_ref[i * per + g, rows, :] for g in range(per)], axis=1)
            )
        total = dot(values[0], weights[0])
        for value, weight in zip(values[1:], weights[1:]):
            total += dot(value, weight)
        total = total.astype(jnp.bfloat16)
        row = 0
        for out_ref in out_refs:
            size = out_ref.shape[0]
            out_ref[:, columns] = total[row : row + size]
            row += size


def call(kernel, name, out_shape, smem, vmem, operands, scratch, limit, flops, anywhere=0):
    specs = [pl.BlockSpec(memory_space=pltpu.SMEM)] * smem
    specs += [pl.BlockSpec(memory_space=pltpu.VMEM)] * vmem
    specs += [pl.BlockSpec(memory_space=pltpu.HBM)] * anywhere
    several = isinstance(out_shape, (tuple, list))
    spec = pl.BlockSpec(memory_space=pltpu.VMEM)
    return pl.pallas_call(
        kernel,
        out_shape=out_shape,
        in_specs=specs,
        out_specs=[spec] * len(out_shape) if several else spec,
        scratch_shapes=scratch,
        compiler_params=pltpu.CompilerParams(vmem_limit_bytes=limit * MIB),
        cost_estimate=pl.CostEstimate(flops=flops, bytes_accessed=4 * MIB, transcendentals=0),
        name=name,
    )(*operands)


def per_device(
    tokens, ln_gain, w_qkv, w_out, w_fc, w_proj, pool_kv, block_table, block_count, lengths
):
    bf16 = jnp.bfloat16
    ring = lax.axis_size("x")
    groups = lax.axis_size("z") * lax.axis_size("core")
    x, y = lax.axis_index("x"), lax.axis_index("y")
    core = lax.axis_index("core")
    group = lax.axis_index("z") * lax.axis_size("core") + core
    place = jnp.stack([x, y, core]).astype(jnp.int32)
    up = [(i, (i + 1) % ring) for i in range(ring)]
    down = [(i, (i - 1) % ring) for i in range(ring)]
    across = [(i, (i + 2) % ring) for i in range(ring)]
    swap = [(0, 1), (1, 0)]

    own = tokens[0]
    part, width = own.shape
    row_tok = part * ring
    group_tok = row_tok * ring
    local_pool = pool_kv[0]
    blk_dev, block_len, _, lanes = local_pool.shape
    pool_blocks = blk_dev * ring * ring
    head = lanes // 2
    units = w_fc.shape[1]
    slab = width // groups

    with jax.named_scope("small_weights"):
        small = jnp.concatenate([w_qkv[:, 0, :].T, w_out[0]], axis=0)
        slices = [
            small,
            lax.ppermute(small, "y", down),
            lax.ppermute(small, "y", across),
            lax.ppermute(small, "y", up),
        ]
        packed = jnp.concatenate(
            [s[head : 3 * head] for s in slices] + [s[:head] for s in slices], axis=0
        )
        qkv_weight = lax.all_gather(packed, ("z", "core"), axis=0, tiled=False)

    normed = layer_norm(own, ln_gain)
    fan = [(i, (i + 1) % ring) for i in range(ring)]
    fan += [(ring + i, ring + (i - 1) % ring) for i in range(ring)]
    with jax.named_scope("gather_tokens"):
        left = lax.ppermute(normed, "x", up)
        right = lax.ppermute(normed, "x", down)
        opposite = lax.ppermute(jnp.where(core == 0, left, right), ("core", "x"), fan)

    def after(value, other):
        return lax.optimization_barrier((value, other))[0]

    with jax.named_scope("far_weights"):
        fc_slab = lax.dynamic_slice_in_dim(after(w_fc, normed), group * slab, slab, 0)
        pieces = [fc_slab[:, b : b + lanes] for b in range(0, units, lanes)]
        proj_slab = lax.dynamic_slice_in_dim(after(w_proj, normed), group * slab, slab, 1)
        payload = jnp.concatenate(pieces + [proj_slab], axis=0)
        far = lax.ppermute(payload, "y", across)

    with jax.named_scope("near_weights"):
        fc_near = lax.ppermute(after(w_fc, payload), ("core", "y"), fan)

    pooled = lax.all_to_all(
        after(local_pool, left), ("y", "x"), split_axis=2, concat_axis=0, tiled=True
    )
    pooled = pooled.reshape(pool_blocks, block_len, lanes)
    cosine, sine = rotation_tables(
        lengths[0], block_count[0], y * row_tok, row_tok, block_len, lanes
    )
    payload = row_tok + row_tok // 2
    sent_shape = jax.ShapeDtypeStruct((payload, lanes), bf16)
    rows, *sent = call(
        functools.partial(qkv_kernel, ring), "qkv",
        [jax.ShapeDtypeStruct((row_tok, width), bf16)] + [sent_shape] * ring,
        1, 0, (place, cosine, sine, normed, right, opposite, left, qkv_weight),
        [
            pltpu.VMEM((groups, 3 * head * ring, lanes), bf16),
            pltpu.VMEM((row_tok, lanes), jnp.float32),
            pltpu.VMEM((row_tok, lanes), jnp.float32),
            pltpu.SemaphoreType.DMA((7,)),
        ],
        56, 3_000 * MIB, 7,
    )
    gathered = lax.all_gather(
        after(
            jnp.concatenate([s[3 * head :] for s in slices] + [far], axis=0),
            (rows, pooled, fc_near),
        ),
        ("z", "core"), axis=0, tiled=False,
    )
    ways = (None, up, across, down)

    def exchange(pieces):
        return [pieces[0]] + [lax.ppermute(p, "y", w) for p, w in zip(pieces[1:], ways[1:])]

    received = exchange(sent)
    work = 2 * row_tok * width * units
    hidden_shape = jax.ShapeDtypeStruct((row_tok, units), bf16)
    work = 2 * row_tok * width * units
    fc_other = lax.ppermute(fc_near, "core", swap)
    (own_hidden,) = call(
        hide_kernel, "hide", [hidden_shape], 0, 2, (rows, w_fc), (), 8, work
    )
    proj_near = lax.ppermute(after(w_proj, tuple(received[1:])), ("core", "y"), fan)

    keys = block_table.shape[2] * block_len
    chunk, tile = 512, 256
    most = -(-(group_tok // 4 + tile + 16) // chunk) * chunk
    heads = call(
        functools.partial(attention_kernel, chunk, tile, head**-0.5, ring), "attend",
        [jax.ShapeDtypeStruct((row_tok // 2, lanes), bf16)] * ring,
        4, 1 + ring, (after(place, own_hidden), block_table[0], block_count[0], lengths[0], pooled, *received),
        [
            pltpu.VMEM((group_tok, lanes), bf16),
            pltpu.VMEM((group_tok + most, lanes), bf16),
            pltpu.VMEM((group_tok + most, lanes), bf16),
            pltpu.VMEM((group_tok, lanes), bf16),
            pltpu.VMEM((keys, lanes), bf16),
            pltpu.VMEM((keys, lanes), bf16),
            pltpu.VMEM((tile, keys + most), jnp.float32),
        ],
        12, 30_000 * MIB,
    )
    proj_other = lax.ppermute(after(proj_near, heads[0]), "core", swap)
    near_hidden, other_hidden = call(
        hide_kernel, "hide_two", [hidden_shape] * 2, 0, 3,
        (after(rows, heads[0]), fc_near, fc_other), (), 8, 2 * work,
    )
    heads = exchange(heads)
    block_shape = jax.ShapeDtypeStruct((part, width), bf16)

    def mix(steps, shapes, given, hide):
        return call(
            functools.partial(mix_kernel, steps, hide), "mix", shapes, 1, 7,
            (
                place, own_hidden, near_hidden, other_hidden,
                heads[0], heads[3], heads[2], heads[1],
                given, w_proj, proj_near, proj_other, gathered,
            ),
            [
                pltpu.VMEM((row_tok, ring * head), bf16),
                pltpu.VMEM(gathered.shape, bf16),
                pltpu.VMEM(given.shape, bf16),
                pltpu.VMEM(w_proj.shape, bf16),
                pltpu.VMEM(w_proj.shape, bf16),
                pltpu.VMEM(w_proj.shape, bf16),
                pltpu.SemaphoreType.DMA((22,)),
            ],
            52, (len(steps) + 2 * hide) * work, 5,
        )

    out2, far_hidden = mix((2,), [block_shape, hidden_shape], rows, True)
    out1, out3, out0 = mix((1, 3, 0), [block_shape] * 3, far_hidden, False)

    with jax.named_scope("reduce_tokens"):
        passed = lax.ppermute(out2, ("core", "x"), fan).astype(jnp.float32)

        def joined(block, which):
            added = jnp.where(core == which, passed, 0.0)
            return (block.astype(jnp.float32) + added).astype(bf16)

        a = lax.ppermute(joined(out1, 0), "x", up).astype(jnp.float32)
        b = lax.ppermute(joined(out3, 1), "x", down).astype(jnp.float32)
    summed = out0.astype(jnp.float32) + a + b
    return (own.astype(jnp.float32) + summed).astype(bf16)[None]


def solution(mesh):
    grid = Mesh(mesh.devices.reshape(8, 2, 4, 4), ("z", "core", "y", "x"))
    grp, pool = ("z", "core"), ("y", "x")
    in_specs = (
        P(grp, pool, None),
        P(),
        P(grp, pool, None),
        P(pool, None, grp),
        P(None, pool),
        P(pool, None),
        P(grp, pool, None, None, None),
        P(grp, None, None),
        P(grp, None),
        P(grp, None),
    )
    return jax.shard_map(
        per_device, mesh=grid, in_specs=in_specs, out_specs=P(grp, pool, None), check_vma=False
    )
```

```python
import functools

import jax
import jax.numpy as jnp
from jax import lax
from jax.experimental import pallas as pl
from jax.experimental.pallas import tpu as pltpu
from jax.sharding import Mesh
from jax.sharding import PartitionSpec as P

ROT = 32
LOG2E = 1.4426950408889634
MIB = 1024 * 1024
epsilon = 1e-05


def layer_norm(rows, gain):
    values = rows.astype(jnp.float32)
    centred = values - jnp.mean(values, axis=-1, keepdims=True)
    variance = jnp.mean(centred * centred, axis=-1, keepdims=True)
    return (centred * lax.rsqrt(variance + epsilon) * gain.astype(jnp.float32)).astype(jnp.bfloat16)


def rotation_tables(request_lengths, counts, first_token, tokens, block_len, lanes):
    half = ROT // 2
    ends = jnp.cumsum(request_lengths)
    starts = ends - request_lengths
    index = first_token + jnp.arange(tokens, dtype=jnp.int32)
    inside = (index[:, None] >= starts[None, :]) & (index[:, None] < ends[None, :])
    position = (
        jnp.sum(jnp.where(inside, (counts * block_len - starts)[None, :], 0), axis=-1) + index
    )
    frequency = 10000.0 ** (-2.0 * jnp.arange(half, dtype=jnp.float32) / ROT)
    lane = jnp.arange(lanes, dtype=jnp.int32)
    spread = jnp.where(lane < ROT, jnp.tile(frequency, lanes // half), 0.0)
    angle = position.astype(jnp.float32)[:, None] * spread[None, :]
    sine = jnp.sin(angle)
    return jnp.cos(angle), jnp.where(lane[None, :] < half, -sine, sine)


def qkv_kernel(
    ring, place_ref, cosine_ref, sine_ref, own_ref, right_ref, opposite_ref, left_ref,
    gathered_ref, rows_ref, *refs
):
    sent_refs, (weight_ref, cos_ref, sin_ref, held_ref, sems) = refs[:ring], refs[ring:]
    x = place_ref[0]
    part = own_ref.shape[0]
    tokens, lanes = cos_ref.shape
    head = lanes // 2

    moves = []
    for step, piece in enumerate((own_ref, right_ref, opposite_ref, left_ref)):
        begin = pl.multiple_of(lax.rem(x + step, ring) * part, part)
        moves.append((piece, held_ref.at[pl.ds(begin, part), :]))
    spans = [(pair * 2 * lanes, 2 * lanes) for pair in range(ring // 2)]
    spans.append((ring * lanes, ring * head))
    for begin, size in spans:
        share = pl.ds(begin, size)
        moves.append((gathered_ref.at[:, share, :], weight_ref.at[:, share, :]))
    moves += [(cosine_ref, cos_ref), (sine_ref, sin_ref), (held_ref, rows_ref)]
    copies = [
        pltpu.make_async_copy(source, target, sems.at[k])
        for k, (source, target) in enumerate(moves)
    ]
    for copy in copies[:-1]:
        copy.start()
    for copy in copies[:ring]:
        copy.wait()
    copies[-1].start()
    lane = lax.broadcasted_iota(jnp.int32, (tokens, lanes), 1)

    def rotated(field):
        other = jnp.where(
            lane < ROT // 2, pltpu.roll(field, lanes - ROT // 2, 1), pltpu.roll(field, ROT // 2, 1)
        )
        return field * cos_ref[...] + other * sin_ref[...]

    def product(k):
        begin, size = spans[k]
        copies[ring + k].wait()
        weight = jnp.concatenate(
            [weight_ref[g, begin : begin + size, :] for g in range(weight_ref.shape[0])], axis=1
        )
        return lax.dot_general(
            held_ref[...], weight, (((1,), (1,)), ((), ())), preferred_element_type=jnp.float32
        )

    for pair in range(ring // 2):
        both = product(pair)
        if pair == 0:
            copies[-3].wait()
            copies[-2].wait()
        for k in range(2):
            field = rotated(both[:, k * lanes : (k + 1) * lanes])
            sent_refs[2 * pair + k][:tokens, :] = field.astype(jnp.bfloat16)
    queries = product(ring // 2)
    for d in range(ring):
        field = queries[:, d // 2 * lanes : (d // 2 + 1) * lanes]
        if d % 2:
            field = pltpu.roll(field, head, 1)
        field = rotated(field)
        top, bottom = field[: tokens // 2], pltpu.roll(field[tokens // 2 :], head, 1)
        folded = jnp.where(lane[: tokens // 2] < head, top, bottom)
        sent_refs[d][tokens:, :] = folded.astype(jnp.bfloat16)
    copies[-1].wait()


def attention_kernel(
    chunk, tile, scale, ring, place_ref, table_ref, count_ref, length_ref, pool_ref, *refs
):
    sent_refs, out_refs = refs[:ring], refs[ring : 2 * ring]
    query_ref, fresh_ref, worth_ref, result_ref, key_ref, value_ref, score_ref = refs[2 * ring :]
    y = place_ref[1]
    tokens, lanes = query_ref.shape
    head = lanes // 2
    part = tokens // ring
    block_len = pool_ref.shape[1]
    requests = table_ref.shape[0]
    per_chunk = chunk // block_len
    factor = scale * LOG2E
    unroll = 8
    block_lane = lax.broadcasted_iota(jnp.int32, (block_len, lanes), 1)
    fold_lane = lax.broadcasted_iota(jnp.int32, (part // 2, lanes), 1)
    part_lane = lax.broadcasted_iota(jnp.int32, (part, lanes), 1)
    one = jnp.ones((), jnp.bfloat16)
    nil = jnp.zeros((), jnp.bfloat16)

    fresh_ref[tokens:, :] = jnp.zeros((fresh_ref.shape[0] - tokens, lanes), jnp.bfloat16)
    worth_ref[tokens:, :] = jnp.zeros((fresh_ref.shape[0] - tokens, lanes), jnp.bfloat16)
    for i in range(ring):
        both = sent_refs[i][:part, :]
        origin = lax.rem(y + ring - i, ring) * part
        block = pl.ds(pl.multiple_of(origin, part), part)
        fresh_ref[block, :] = both
        worth_ref[block, :] = jnp.where(part_lane < head, one, both)
        folded = sent_refs[i][part:, :].astype(jnp.float32)
        for k in range(2):
            unfolded = folded if k == 0 else pltpu.roll(folded, head, 1)
            begin = pl.multiple_of(origin + k * (part // 2), part // 2)
            query_ref[pl.ds(begin, part // 2), :] = jnp.where(
                fold_lane < head, unfolded, 0.0
            ).astype(jnp.bfloat16)

    def dot_t(a, b):
        return lax.dot_general(a, b, (((1,), (1,)), ((), ())), preferred_element_type=jnp.float32)

    def peak(highest, scores):
        for k in range(0, scores.shape[1], lanes):
            highest = jnp.maximum(highest, scores[:, k : k + lanes])
        return highest

    def request(r, start):
        length = length_ref[r]
        count = count_ref[r]
        chunks = (count + per_chunk - 1) // per_chunk
        pairs = chunks // 2

        def gather(i, _):
            for u in range(unroll):
                b = i * unroll + u
                block = pool_ref[table_ref[r, jnp.minimum(b, count - 1)]]
                where = pl.ds(pl.multiple_of(b * block_len, block_len), block_len)
                key_ref[where, :] = block
                paired = jnp.where(block_lane < head, one, block)
                value_ref[where, :] = jnp.where(b < count, paired, nil)
            return 0

        lax.fori_loop(0, chunks * (per_chunk // unroll), gather, 0)
        first = start // 16 * 16
        tiles = (start + length - first + tile - 1) // tile

        def one_tile(i, _):
            row = pl.multiple_of(jnp.minimum(first + i * tile, tokens - tile), 16)
            rows = pl.ds(row, tile)
            query = query_ref[rows, :]
            fresh_chunks = (row + tile - first + chunk - 1) // chunk
            own = row + lax.broadcasted_iota(jnp.int32, (tile, chunk), 0)
            column = first + lax.broadcasted_iota(jnp.int32, (tile, chunk), 1)

            def at(j):
                return pl.ds(pl.multiple_of(j * chunk, chunk), chunk)

            def fresh_at(j):
                return pl.ds(pl.multiple_of(first + j * chunk, 16), chunk)

            def look(size):
                def body(j, highest):
                    where = pl.ds(pl.multiple_of(j * size, size), size)
                    scores = dot_t(query, key_ref[where, :])
                    score_ref[:, where] = scores
                    return peak(highest, scores)

                return body

            def look_fresh(j, highest):
                scores = dot_t(query, fresh_ref[fresh_at(j), :])
                other = column + j * chunk
                visible = (other >= start) & (other <= own)
                scores = jnp.where(visible, scores, -1e30)
                score_ref[:, at(chunks + j)] = scores
                return peak(highest, scores)

            highest = jnp.full((tile, lanes), -1e30, jnp.float32)
            highest = lax.fori_loop(0, pairs, look(2 * chunk), highest)
            highest = lax.fori_loop(2 * pairs, chunks, look(chunk), highest)
            highest = lax.fori_loop(0, fresh_chunks, look_fresh, highest)
            top = factor * jnp.max(highest, axis=-1, keepdims=True)

            def weigh(size):
                def body(j, acc):
                    where = pl.ds(pl.multiple_of(j * size, size), size)
                    weights = jnp.exp2(factor * score_ref[:, where] - top).astype(jnp.bfloat16)
                    return acc + dot(weights, value_ref[where, :])

                return body

            def weigh_fresh(j, acc):
                weights = jnp.exp2(factor * score_ref[:, at(chunks + j)] - top).astype(jnp.bfloat16)
                return acc + jnp.dot(
                    weights, worth_ref[fresh_at(j), :], preferred_element_type=jnp.float32
                )

            acc = jnp.zeros((tile, lanes), jnp.float32)
            acc = lax.fori_loop(0, pairs, weigh(2 * chunk), acc)
            acc = lax.fori_loop(2 * pairs, chunks, weigh(chunk), acc)
            acc = lax.fori_loop(0, fresh_chunks, weigh_fresh, acc)
            result = (acc / pltpu.roll(acc, head, 1)).astype(jnp.bfloat16)
            place = row + lax.broadcasted_iota(jnp.int32, (tile, lanes), 0)
            inside = (place >= start) & (place < start + length)
            result_ref[rows, :] = jnp.where(inside, result, result_ref[rows, :])
            return 0

        lax.fori_loop(0, tiles, one_tile, 0)
        return start + length

    lax.fori_loop(0, requests, request, 0)
    for i in range(ring):
        begin = pl.multiple_of(lax.rem(y + i, ring) * part, part)
        top = result_ref[pl.ds(begin, part // 2), :].astype(jnp.float32)
        bottom = result_ref[pl.ds(begin + part // 2, part // 2), :].astype(jnp.float32)
        out_refs[i][...] = jnp.where(fold_lane < head, pltpu.roll(top, head, 1), bottom).astype(
            jnp.bfloat16
        )


def gelu(value):
    return jax.nn.gelu(value, approximate=True).astype(jnp.bfloat16)


def dot(a, b):
    return jnp.dot(a, b, preferred_element_type=jnp.float32)


def hide_kernel(rows_ref, *refs):
    half = len(refs) // 2
    for fc_ref, hidden_ref in zip(refs[:half], refs[half:]):
        hidden_ref[...] = gelu(dot(rows_ref[...], fc_ref[...]))


def mix_kernel(
    steps, hide, place_ref, own_ref, near_ref, other_ref,
    head0_ref, head1_ref, head2_ref, head3_ref,
    given_ref, proj_own_hbm, proj_near_hbm, proj_other_hbm, gathered_ref, *refs
):
    out_refs, refs = refs[:-7], refs[-7:]
    attention_ref, held_ref, far_ref, proj_own_ref, proj_near_ref, proj_other_ref, sems = refs
    x = place_ref[0]
    tokens, units = own_ref.shape
    width = proj_own_ref.shape[1]
    groups, held, lanes = gathered_ref.shape
    begin = held - 2 * units
    head = lanes // 2
    ring = attention_ref.shape[1] // head
    part = tokens // ring
    stripe = 512

    per = stripe // lanes
    moves = [(given_ref, far_ref)]
    if hide:
        moves.append(
            (gathered_ref.at[:, pl.ds(begin, units), :], held_ref.at[:, pl.ds(begin, units), :])
        )
    ready = len(moves)
    for i in range(width // stripe):
        columns, share = pl.ds(i * stripe, stripe), pl.ds(i * per, per)
        for source, target in (
            (proj_own_hbm, proj_own_ref), (proj_near_hbm, proj_near_ref),
            (proj_other_hbm, proj_other_ref),
        ):
            moves.append((source.at[:, columns], target.at[:, columns]))
        for rows in (pl.ds(held - units, units), pl.ds(0, begin)):
            moves.append((gathered_ref.at[share, rows, :], held_ref.at[share, rows, :]))
    copies = [
        pltpu.make_async_copy(source, target, sems.at[k])
        for k, (source, target) in enumerate(moves)
    ]
    for copy in copies:
        copy.start()
    fold_lane = lax.broadcasted_iota(jnp.int32, (tokens // 2, lanes), 1)
    for k, (first, second) in enumerate(((head0_ref, head1_ref), (head2_ref, head3_ref))):
        a, b = first[...].astype(jnp.float32), second[...].astype(jnp.float32)
        columns = slice(k * lanes, (k + 1) * lanes)
        attention_ref[: tokens // 2, columns] = jnp.where(
            fold_lane < head, a, pltpu.roll(b, head, 1)
        ).astype(jnp.bfloat16)
        attention_ref[tokens // 2 :, columns] = jnp.where(
            fold_lane < head, pltpu.roll(a, head, 1), b
        ).astype(jnp.bfloat16)

    def take(ref):
        return jnp.concatenate(
            [
                ref[pl.ds(pl.multiple_of(lax.rem(x + step, ring) * part, part), part), :]
                for step in steps
            ],
            axis=0,
        )

    for copy in copies[:ready]:
        copy.wait()
    if hide:
        fc = jnp.concatenate(
            [
                jnp.concatenate(
                    [
                        held_ref[g, begin + b * lanes : begin + (b + 1) * lanes, :]
                        for b in range(units // lanes)
                    ],
                    axis=1,
                )
                for g in range(groups)
            ],
            axis=0,
        )
        out_refs[-1][...] = gelu(dot(far_ref[...], fc))
        far_ref, out_refs = out_refs[-1], out_refs[:-1]
    values = [take(ref) for ref in (own_ref, near_ref, other_ref, far_ref, attention_ref)]
    for i in range(width // stripe):
        for copy in copies[ready + 5 * i : ready + 5 * (i + 1)]:
            copy.wait()
        columns = slice(i * stripe, (i + 1) * stripe)
        weights = [ref[:, columns] for ref in (proj_own_ref, proj_near_ref, proj_other_ref)]
        for rows in (slice(held - units, held), slice(0, ring * head)):
            weights.append(
                jnp.concatenate([held_ref[i * per + g, rows, :] for g in range(per)], axis=1)
            )
        total = dot(values[0], weights[0])
        for value, weight in zip(values[1:], weights[1:]):
            total += dot(value, weight)
        total = total.astype(jnp.bfloat16)
        row = 0
        for out_ref in out_refs:
            size = out_ref.shape[0]
            out_ref[:, columns] = total[row : row + size]
            row += size


def call(kernel, name, out_shape, smem, vmem, operands, scratch, limit, flops, anywhere=0, far_outs=()):
    specs = [pl.BlockSpec(memory_space=pltpu.SMEM)] * smem
    specs += [pl.BlockSpec(memory_space=pltpu.VMEM)] * vmem
    specs += [pl.BlockSpec(memory_space=pltpu.HBM)] * anywhere
    several = isinstance(out_shape, (tuple, list))
    spec = pl.BlockSpec(memory_space=pltpu.VMEM)
    return pl.pallas_call(
        kernel,
        out_shape=out_shape,
        in_specs=specs,
        out_specs=[
            pl.BlockSpec(memory_space=pltpu.HBM) if k in far_outs else spec
            for k in range(len(out_shape))
        ] if several else spec,
        scratch_shapes=scratch,
        compiler_params=pltpu.CompilerParams(vmem_limit_bytes=limit * MIB),
        cost_estimate=pl.CostEstimate(flops=flops, bytes_accessed=4 * MIB, transcendentals=0),
        name=name,
    )(*operands)


def per_device(
    tokens, ln_gain, w_qkv, w_out, w_fc, w_proj, pool_kv, block_table, block_count, lengths
):
    bf16 = jnp.bfloat16
    ring = lax.axis_size("x")
    groups = lax.axis_size("z") * lax.axis_size("core")
    x, y = lax.axis_index("x"), lax.axis_index("y")
    core = lax.axis_index("core")
    group = lax.axis_index("z") * lax.axis_size("core") + core
    place = jnp.stack([x, y, core]).astype(jnp.int32)
    up = [(i, (i + 1) % ring) for i in range(ring)]
    down = [(i, (i - 1) % ring) for i in range(ring)]
    across = [(i, (i + 2) % ring) for i in range(ring)]
    swap = [(0, 1), (1, 0)]

    own = tokens[0]
    part, width = own.shape
    row_tok = part * ring
    group_tok = row_tok * ring
    local_pool = pool_kv[0]
    blk_dev, block_len, _, lanes = local_pool.shape
    pool_blocks = blk_dev * ring * ring
    head = lanes // 2
    units = w_fc.shape[1]
    slab = width // groups

    with jax.named_scope("small_weights"):
        small = jnp.concatenate([w_qkv[:, 0, :].T, w_out[0]], axis=0)
        slices = [
            small,
            lax.ppermute(small, "y", down),
            lax.ppermute(small, "y", across),
            lax.ppermute(small, "y", up),
        ]
        packed = jnp.concatenate(
            [s[head : 3 * head] for s in slices] + [s[:head] for s in slices], axis=0
        )
        qkv_weight = lax.all_gather(packed, ("z", "core"), axis=0, tiled=False)

    normed = layer_norm(own, ln_gain)
    fan = [(i, (i + 1) % ring) for i in range(ring)]
    fan += [(ring + i, ring + (i - 1) % ring) for i in range(ring)]
    with jax.named_scope("gather_tokens"):
        left = lax.ppermute(normed, "x", up)
        right = lax.ppermute(normed, "x", down)
        opposite = lax.ppermute(jnp.where(core == 0, left, right), ("core", "x"), fan)

    def after(value, other):
        return lax.optimization_barrier((value, other))[0]

    with jax.named_scope("far_weights"):
        fc_slab = lax.dynamic_slice_in_dim(after(w_fc, normed), group * slab, slab, 0)
        pieces = [fc_slab[:, b : b + lanes] for b in range(0, units, lanes)]
        proj_slab = lax.dynamic_slice_in_dim(after(w_proj, normed), group * slab, slab, 1)
        payload = jnp.concatenate(pieces + [proj_slab], axis=0)
        far = lax.ppermute(payload, "y", across)

    with jax.named_scope("near_weights"):
        fc_near = lax.ppermute(after(w_fc, payload), ("core", "y"), fan)

    pooled = lax.all_to_all(
        after(local_pool, left), ("y", "x"), split_axis=2, concat_axis=0, tiled=True
    )
    pooled = pooled.reshape(pool_blocks, block_len, lanes)
    cosine, sine = rotation_tables(
        lengths[0], block_count[0], y * row_tok, row_tok, block_len, lanes
    )
    payload = row_tok + row_tok // 2
    sent_shape = jax.ShapeDtypeStruct((payload, lanes), bf16)
    rows, *sent = call(
        functools.partial(qkv_kernel, ring), "qkv",
        [jax.ShapeDtypeStruct((row_tok, width), bf16)] + [sent_shape] * ring,
        1, 0, (place, cosine, sine, normed, right, opposite, left, qkv_weight),
        [
            pltpu.VMEM((groups, 3 * head * ring, lanes), bf16),
            pltpu.VMEM((row_tok, lanes), jnp.float32),
            pltpu.VMEM((row_tok, lanes), jnp.float32),
            pltpu.VMEM((row_tok, width), bf16),
            pltpu.SemaphoreType.DMA((10,)),
        ],
        56, 3_000 * MIB, 7, (0,),
    )
    gathered = lax.all_gather(
        after(
            jnp.concatenate([s[3 * head :] for s in slices] + [far], axis=0),
            (rows, pooled, fc_near),
        ),
        ("z", "core"), axis=0, tiled=False,
    )
    ways = (None, up, across, down)

    def exchange(pieces):
        return [pieces[0]] + [lax.ppermute(p, "y", w) for p, w in zip(pieces[1:], ways[1:])]

    received = exchange(sent)
    work = 2 * row_tok * width * units
    hidden_shape = jax.ShapeDtypeStruct((row_tok, units), bf16)
    work = 2 * row_tok * width * units
    fc_other = lax.ppermute(fc_near, "core", swap)
    (own_hidden,) = call(
        hide_kernel, "hide", [hidden_shape], 0, 2, (rows, w_fc), (), 8, work
    )
    proj_near = lax.ppermute(after(w_proj, tuple(received[1:])), ("core", "y"), fan)

    keys = block_table.shape[2] * block_len
    chunk, tile = 512, 256
    most = -(-(group_tok // 4 + tile + 16) // chunk) * chunk
    heads = call(
        functools.partial(attention_kernel, chunk, tile, head**-0.5, ring), "attend",
        [jax.ShapeDtypeStruct((row_tok // 2, lanes), bf16)] * ring,
        4, 1 + ring, (after(place, own_hidden), block_table[0], block_count[0], lengths[0], pooled, *received),
        [
            pltpu.VMEM((group_tok, lanes), bf16),
            pltpu.VMEM((group_tok + most, lanes), bf16),
            pltpu.VMEM((group_tok + most, lanes), bf16),
            pltpu.VMEM((group_tok, lanes), bf16),
            pltpu.VMEM((keys, lanes), bf16),
            pltpu.VMEM((keys, lanes), bf16),
            pltpu.VMEM((tile, keys + most), jnp.float32),
        ],
        12, 30_000 * MIB,
    )
    proj_other = lax.ppermute(after(proj_near, heads[0]), "core", swap)
    near_hidden, other_hidden = call(
        hide_kernel, "hide_two", [hidden_shape] * 2, 0, 3,
        (after(rows, heads[0]), fc_near, fc_other), (), 8, 2 * work,
    )
    heads = exchange(heads)
    block_shape = jax.ShapeDtypeStruct((part, width), bf16)

    def mix(steps, shapes, given, hide):
        return call(
            functools.partial(mix_kernel, steps, hide), "mix", shapes, 1, 7,
            (
                place, own_hidden, near_hidden, other_hidden,
                heads[0], heads[3], heads[2], heads[1],
                given, w_proj, proj_near, proj_other, gathered,
            ),
            [
                pltpu.VMEM((row_tok, ring * head), bf16),
                pltpu.VMEM(gathered.shape, bf16),
                pltpu.VMEM(given.shape, bf16),
                pltpu.VMEM(w_proj.shape, bf16),
                pltpu.VMEM(w_proj.shape, bf16),
                pltpu.VMEM(w_proj.shape, bf16),
                pltpu.SemaphoreType.DMA((22,)),
            ],
            52, (len(steps) + 2 * hide) * work, 5,
        )

    out2, far_hidden = mix((2,), [block_shape, hidden_shape], rows, True)
    out1, out3, out0 = mix((1, 3, 0), [block_shape] * 3, far_hidden, False)

    with jax.named_scope("reduce_tokens"):
        passed = lax.ppermute(out2, ("core", "x"), fan).astype(jnp.float32)

        def joined(block, which):
            added = jnp.where(core == which, passed, 0.0)
            return (block.astype(jnp.float32) + added).astype(bf16)

        a = lax.ppermute(joined(out1, 0), "x", up).astype(jnp.float32)
        b = lax.ppermute(joined(out3, 1), "x", down).astype(jnp.float32)
    summed = out0.astype(jnp.float32) + a + b
    return (own.astype(jnp.float32) + summed).astype(bf16)[None]


def solution(mesh):
    grid = Mesh(mesh.devices.reshape(8, 2, 4, 4), ("z", "core", "y", "x"))
    grp, pool = ("z", "core"), ("y", "x")
    in_specs = (
        P(grp, pool, None),
        P(),
        P(grp, pool, None),
        P(pool, None, grp),
        P(None, pool),
        P(pool, None),
        P(grp, pool, None, None, None),
        P(grp, None, None),
        P(grp, None),
        P(grp, None),
    )
    return jax.shard_map(
        per_device, mesh=grid, in_specs=in_specs, out_specs=P(grp, pool, None), check_vma=False
    )
```
